32 devices in a mesh: groups: 2 (over x), tm: 16 (over z, y, core).
Axes of the slice: x: 2, y: 2, z: 4, core: 2. Of those that a mesh axis runs over, the one named last changes fastest.
Arguments:
- features: bfloat16 [32768, 80], P(('groups', 'tm')), parts along dimension 0, may hold values from -6 to 6
- stem_kernel: bfloat16 [3, 3, 256], replicated, may hold values from -3 to 3
- mid_depthwise: bfloat16 [3, 3, 256], replicated, may hold values from -3 to 3
- mid_pointwise: bfloat16 [256, 256], replicated, may hold values from -0.5 to 0.5
- last_depthwise: bfloat16 [3, 3, 256], replicated, may hold values from -3 to 3
- last_pointwise: bfloat16 [256, 256], replicated, may hold values from -0.5 to 0.5
- proj_weight: bfloat16 [2560, 1024], replicated, may hold values from -0.15625 to 0.15625
- norm_gain: float32 [1024], replicated, may hold values from 0.25 to 1.75
- qkv_weight: bfloat16 [1024, 3072], replicated
- out_weight: bfloat16 [1024, 1024], replicated, may hold values from -0.1875 to 0.1875
- cotangent: bfloat16 [4096, 1024], P(('groups', 'tm')), parts along dimension 0, may hold values from -6 to 6
- utt_bounds: int32 [16, 2], P('groups'), parts along dimension 0, may hold values from 0 to 2048, as said below
- live_blocks: int32 [32, 7], P(('groups', 'tm')), parts along dimension 0, may hold values from 0 to 1, as said below
Outputs:
- block_out: bfloat16 [4096, 1024], P(('groups', 'tm')), parts along dimension 0
- frame_grads: bfloat16 [4096, 1024], P(('groups', 'tm')), parts along dimension 0
- proj_grads: float32 [5120, 1024], P(('groups', 'tm')), parts along dimension 0
The draws below stay inside these ranges and needn't reach their ends.
There are 2 independent parts, one for each index of `groups`. The reference program is written for one: setup_inputs(seed, part) draws one part's arguments, and reference() takes and returns one part's arrays. A program takes and returns all parts, laid end to end along the dimension named above; an argument that names none is the same for every part. Nothing has to cross between parts.
Inputs may be any that keep to these rules, and one draw needn't show every extreme that they name: `utt_bounds`: rows are in order of time and tile frames 0 to 2048 without gaps; each utterance has 1 to 384 frames and one has exactly 384. `live_blocks`: entry [b, c] is 1 iff some utterance has frames in block b (frames b * 128 to (b + 1) * 128 - 1) and in block b + c - 3; it is 0 where that block lies outside the recording.
All inputs are finite; a program needn't handle non-finite values.
Results may differ from the reference program's by a relative error of at most 0.015.
Values may be sent and summed in bfloat16 or wider, within the bound.
A program may use at most 128 MiB of HBM per device.

```python
import math
import jax
import jax.numpy as jnp
from jax import lax

D = 1024
HEADS = 8
CHANNELS = 256
MEL = 80
FRAME_DEV = 128
REACH = 3
HEAD_DIM = 128
PROJ_IN = 2560
FRAMES = 2048
FEAT_ROWS = 16384
MAXLEN = 384
UTTS = 8


def utterance_bounds(key):
    base_key = jax.random.fold_in(key, 7)
    order_key, weight_key = jax.random.split(base_key)
    spare_frames = FRAMES - UTTS
    full_count = spare_frames // (MAXLEN - 1)
    short_count = UTTS - full_count
    remaining = spare_frames - full_count * (MAXLEN - 1)
    weights = jax.random.randint(weight_key, (short_count,), 32, 64)
    extra_frames = remaining * weights // jnp.sum(weights)
    leftover = remaining - jnp.sum(extra_frames)
    positions = jnp.arange(short_count)
    short_lengths = 1 + extra_frames + (positions < leftover).astype(jnp.int32)
    full_lengths = jnp.full((full_count,), MAXLEN, jnp.int32)
    all_lengths = jnp.concatenate([full_lengths, short_lengths.astype(jnp.int32)])
    order = jax.random.permutation(order_key, UTTS)
    lengths = all_lengths[order]
    utt_ends = jnp.cumsum(lengths)
    starts = utt_ends - lengths
    return jnp.stack([starts, utt_ends], axis=1).astype(jnp.int32)


def segment_at(positions, bounds):
    return jnp.sum((bounds[None, :, 0] <= positions[:, None]).astype(jnp.int32), axis=1) - 1


def draw_utt_bounds(key, part):
    return utterance_bounds(key)


def draw_live_blocks(key, part):
    bounds = utterance_bounds(key)
    blocks = FRAMES // FRAME_DEV
    firsts = jnp.arange(blocks) * FRAME_DEV
    block_lasts = firsts + FRAME_DEV - 1
    seg_first = segment_at(firsts, bounds)
    seg_last = segment_at(block_lasts, bounds)
    offsets = jnp.arange(2 * REACH + 1) - REACH
    partner = jnp.arange(blocks)[:, None] + offsets[None, :]
    inside = (partner >= 0) & (partner < blocks)
    clipped = jnp.clip(partner, 0, blocks - 1)
    forward_share = seg_last[:, None] == seg_first[clipped]
    earlier = seg_first[:, None] == seg_last[clipped]
    shared = jnp.where(offsets[None, :] > 0, forward_share, jnp.where(offsets[None, :] < 0, earlier, True)) & inside
    return shared.astype(jnp.int32)


def draw_qkv_weight(key, part):
    weights = jax.random.normal(jax.random.fold_in(key, 11), (D, 3 * D), jnp.float32) / math.sqrt(D)
    head_factor = jax.random.uniform(jax.random.fold_in(key, 13), (HEADS,), jnp.float32, 2.0, 3.5)
    column = jnp.arange(D)
    head_of = column // HEAD_DIM
    column_factor = head_factor[head_of]
    query_part = weights[:, :D] * column_factor[None, :]
    return jnp.concatenate([query_part, weights[:, D:]], axis=1).astype(jnp.bfloat16)


def block_levels(rng, shape, cuts, least, top_value):
    loudness = 1.0
    for dim, blocks in cuts:
        heights = jax.random.uniform(jax.random.fold_in(jax.random.fold_in(rng, 6), dim), (blocks,), jnp.float32, least / len(cuts), top_value / len(cuts))
        loudness = loudness * jnp.repeat(jnp.exp(heights), shape[dim] // blocks).reshape((-1,) + (1,) * (len(shape) - 1 - dim))
    return loudness


def gaussian(own_key, extent, width, most, pieces=(), kind=jnp.bfloat16):
    loudness = block_levels(own_key, extent, pieces, -0.22, 0.18) if pieces else 1.0
    entries = jax.random.normal(own_key, extent, jnp.float32) * width * loudness
    return jnp.minimum(jnp.maximum(entries, -most), most).astype(kind)


def setup_inputs(seed: int = 0, part: int = 0) -> dict:
    seeds = jax.random.split(jax.random.key(seed), 14)
    part_splits = jax.random.split(jax.random.fold_in(seeds[13], part), 14)
    return {
        "features": gaussian(part_splits[0], (FEAT_ROWS, MEL), 1.0, 6.0, ((0, 16),)),
        "stem_kernel": gaussian(seeds[1], (3, 3, CHANNELS), 4 ** -0.5, 3.0),
        "mid_depthwise": gaussian(seeds[2], (3, 3, CHANNELS), 4 ** -0.5, 3.0),
        "mid_pointwise": gaussian(seeds[3], (CHANNELS, CHANNELS), (CHANNELS // 2) ** -0.5, 0.5),
        "last_depthwise": gaussian(seeds[4], (3, 3, CHANNELS), 4 ** -0.5, 3.0),
        "last_pointwise": gaussian(seeds[5], (CHANNELS, CHANNELS), (CHANNELS // 2) ** -0.5, 0.5),
        "proj_weight": gaussian(seeds[6], (PROJ_IN, D), (PROJ_IN // 2) ** -0.5, 0.15625),
        "norm_gain": jnp.clip(1.0 + 0.15 * jax.random.normal(seeds[7], (D,), jnp.float32), 0.25, 1.75),
        "qkv_weight": draw_qkv_weight(jax.random.fold_in(seeds[13], 71), part),
        "out_weight": gaussian(seeds[9], (D, D), D ** -0.5, 0.1875),
        "cotangent": gaussian(part_splits[10], (FRAMES, D), 1.0, 6.0, ((0, 16),)),
        "utt_bounds": draw_utt_bounds(jax.random.fold_in(jax.random.fold_in(seeds[13], part), 71), part),
        "live_blocks": draw_live_blocks(jax.random.fold_in(jax.random.fold_in(seeds[13], part), 71), part),
    }


norm_eps = 1e-05
neg_fill = -1e+30

def rounded(values):
    return lax.optimization_barrier(values.astype(jnp.bfloat16)).astype(jnp.float32)

def conv_same(inputs, kernel, groups):
    result = lax.conv_general_dilated(inputs[None], kernel, (2, 2), ((1, 1), (1, 1)), dimension_numbers=('NHWC', 'HWIO', 'NHWC'), feature_group_count=groups, preferred_element_type=jnp.float32)
    return result[0]

def pointwise(depth_out, weight):
    in_shape = depth_out.shape
    mixed_rows = jnp.dot(depth_out.reshape(-1, in_shape[-1]), weight, preferred_element_type=jnp.float32)
    return jax.nn.relu(mixed_rows).reshape(in_shape[:-1] + (weight.shape[1],)).astype(jnp.bfloat16)

def segment_of(positions, utt_bounds):
    inside = (utt_bounds[None, :, 0] <= positions[:, None]) & (positions[:, None] < utt_bounds[None, :, 1])
    number = jnp.arange(utt_bounds.shape[0], dtype=jnp.int32)
    found = lax.optimization_barrier(jnp.sum(jnp.where(inside, number[None, :], 0), axis=1)).astype(jnp.int32)
    return jnp.where(jnp.any(inside, axis=1), found, -1).astype(jnp.int32)

def reference(features, stem_kernel, mid_depthwise, mid_pointwise, last_depthwise, last_pointwise, proj_weight, norm_gain, qkv_weight, out_weight, cotangent, utt_bounds, live_blocks):
    channels = stem_kernel.shape[-1]
    first_section = jax.nn.relu(conv_same(features[:, :, None], stem_kernel[:, :, None, :], 1)).astype(jnp.bfloat16)
    mid_depth = conv_same(first_section, mid_depthwise[:, :, None, :], channels).astype(jnp.bfloat16)
    second_section = pointwise(mid_depth, mid_pointwise)
    last_depth = conv_same(second_section, last_depthwise[:, :, None, :], channels).astype(jnp.bfloat16)
    third_section = pointwise(last_depth, last_pointwise)
    flat_rows = third_section.reshape(FRAMES, PROJ_IN)
    frames = jnp.dot(flat_rows, proj_weight, preferred_element_type=jnp.float32).astype(jnp.bfloat16)
    frames_f = frames.astype(jnp.float32)
    row_mean = lax.optimization_barrier(jnp.mean(frames_f, axis=-1, keepdims=True))
    centered = frames_f - row_mean
    inv_std = lax.rsqrt(lax.optimization_barrier(jnp.mean(centered * centered, axis=-1, keepdims=True)) + norm_eps)
    normalized = centered * inv_std
    normed = (normalized * norm_gain.astype(jnp.float32)).astype(jnp.bfloat16)
    projected = jnp.dot(normed, qkv_weight, preferred_element_type=jnp.float32).astype(jnp.bfloat16)
    score_scale = HEAD_DIM ** (-0.5)
    query_heads = projected[:, :D].astype(jnp.float32).reshape(FRAMES, HEADS, HEAD_DIM)
    key_pad = jnp.pad(projected[:, D:2 * D].astype(jnp.float32), ((MAXLEN, MAXLEN), (0, 0))).reshape(-1, HEADS, HEAD_DIM)
    value_pad = jnp.pad(projected[:, 2 * D:].astype(jnp.float32), ((MAXLEN, MAXLEN), (0, 0))).reshape(-1, HEADS, HEAD_DIM)
    segments = segment_of(jnp.arange(FRAMES, dtype=jnp.int32), utt_bounds)
    segment_pad = jnp.pad(segments, (MAXLEN, MAXLEN), constant_values=-1)
    query_block = math.gcd(FRAMES, 512)
    key_window = query_block + 2 * MAXLEN
    block_starts = jnp.arange(FRAMES // query_block, dtype=jnp.int32) * query_block

    def window_scores(row_start):
        query_pos = row_start + jnp.arange(query_block, dtype=jnp.int32)
        key_pos = row_start - MAXLEN + jnp.arange(key_window, dtype=jnp.int32)
        query_seg = lax.dynamic_slice_in_dim(segments, row_start, query_block)
        key_seg = lax.dynamic_slice_in_dim(segment_pad, row_start, key_window)
        query_blk = query_pos // FRAME_DEV
        offsets = ((key_pos + MAXLEN) // FRAME_DEV - REACH)[None, :] - query_blk[:, None]
        block_flags = live_blocks[query_blk[:, None], jnp.clip(offsets + REACH, 0, 2 * REACH)]
        allowed = (query_seg[:, None] == key_seg[None, :]) & (jnp.abs(offsets) <= REACH) & (block_flags == 1)
        query_part = lax.dynamic_slice_in_dim(query_heads, row_start, query_block)
        key_part = lax.dynamic_slice_in_dim(key_pad, row_start, key_window)
        value_part = lax.dynamic_slice_in_dim(value_pad, row_start, key_window)
        scores = jnp.einsum('qhd,khd->hqk', query_part, key_part) * score_scale
        return (jnp.where(allowed[None], scores, neg_fill), query_part, key_part, value_part)

    def forward_block(row_start):
        scores, query_part, key_part, value_part = window_scores(row_start)
        row_max = lax.optimization_barrier(jnp.max(scores, axis=-1))
        log_norm = row_max + jnp.log(lax.optimization_barrier(jnp.sum(jnp.exp(scores - row_max[..., None]), axis=-1)))
        probs = rounded(jnp.exp(scores - log_norm[..., None]))
        mixed_heads = jnp.einsum('hqk,khd->qhd', probs, value_part)
        return (mixed_heads.reshape(query_block, D).astype(jnp.bfloat16), log_norm)
    attention_blocks, log_norms = lax.map(forward_block, block_starts)
    attention = attention_blocks.reshape(FRAMES, D)
    block_out = (frames_f + jnp.dot(attention, out_weight, preferred_element_type=jnp.float32)).astype(jnp.bfloat16)
    d_attention = jnp.dot(cotangent, out_weight.T, preferred_element_type=jnp.float32).astype(jnp.bfloat16)
    d_heads = d_attention.astype(jnp.float32).reshape(FRAMES, HEADS, HEAD_DIM)
    delta = lax.optimization_barrier(jnp.sum(d_heads * attention.astype(jnp.float32).reshape(FRAMES, HEADS, HEAD_DIM), axis=-1))

    def backward_block(carried, inputs_now):
        row_start, log_norm = inputs_now
        scores, query_part, key_part, value_part = window_scores(row_start)
        dout_part = lax.dynamic_slice_in_dim(d_heads, row_start, query_block)
        delta_part = lax.dynamic_slice_in_dim(delta, row_start, query_block).T
        weights_full = jnp.exp(scores - log_norm[..., None])
        dprob = jnp.einsum('qhd,khd->hqk', dout_part, value_part)
        dscore = rounded(weights_full * (dprob - delta_part[..., None]))
        grad_rows = (score_scale * jnp.einsum('hqk,khd->qhd', dscore, key_part)).reshape(query_block, D).astype(jnp.bfloat16)
        grad_keys = score_scale * jnp.einsum('hqk,qhd->khd', dscore, query_part)
        grad_values = jnp.einsum('hqk,qhd->khd', rounded(weights_full), dout_part)
        both_grads = jnp.stack([grad_keys, grad_values]).reshape(2, key_window, D)
        current = lax.dynamic_slice_in_dim(carried, row_start, key_window, axis=1)
        carried = lax.dynamic_update_slice_in_dim(carried, current + both_grads, row_start, axis=1)
        return (carried, grad_rows)
    start_sums = jnp.zeros((2, FRAMES + 2 * MAXLEN, D), jnp.float32)
    key_sums, grad_blocks = lax.scan(backward_block, start_sums, (block_starts, log_norms))
    grad_query = grad_blocks.reshape(FRAMES, D)
    grad_key = key_sums[0, MAXLEN:MAXLEN + FRAMES].astype(jnp.bfloat16)
    grad_value = key_sums[1, MAXLEN:MAXLEN + FRAMES].astype(jnp.bfloat16)
    grad_normed = jnp.dot(jnp.concatenate([grad_query, grad_key, grad_value], axis=1), qkv_weight.T, preferred_element_type=jnp.float32)
    scaled_grad = grad_normed * norm_gain.astype(jnp.float32)
    ln_grad = inv_std * (scaled_grad - lax.optimization_barrier(jnp.mean(scaled_grad, axis=-1, keepdims=True)) - normalized * lax.optimization_barrier(jnp.mean(scaled_grad * normalized, axis=-1, keepdims=True)))
    frame_grads = (cotangent.astype(jnp.float32) + ln_grad).astype(jnp.bfloat16)
    proj_grads = jnp.dot(flat_rows.T, frame_grads, preferred_element_type=jnp.float32)
    return (block_out, frame_grads, proj_grads)
```

```python
import functools

import jax
import jax.numpy as jnp
from jax import lax
from jax.experimental import pallas as pl
from jax.experimental.pallas import tpu as pltpu
from jax.sharding import PartitionSpec as P

HEADS = 8
REACH = 3
HEAD_DIM = 128
norm_eps = 1e-05
neg_fill = -1e30
MEL_PITCH = 84
SCALE = HEAD_DIM ** (-0.5)


def dot_nt(a, b):
    return lax.dot_general(a, b, (((1,), (1,)), ((), ())), preferred_element_type=jnp.float32)


def dot_tn(a, b):
    return lax.dot_general(a, b, (((0,), (0,)), ((), ())), preferred_element_type=jnp.float32)


def dot_nn(a, b):
    return jnp.dot(a, b, preferred_element_type=jnp.float32)


MESH = pl.DeviceIdType.MESH


class Exchange:
    def __init__(self, size, x_ref, out_ref, send, recv):
        self.size, self.x, self.out, self.send, self.recv = size, x_ref, out_ref, send, recv
        self.me = lax.axis_index("tm")
        self.odd = lax.rem(self.me, 2)
        self.sibling = self.me + 1 - 2 * self.odd
        self.far = self.me - 3 + 6 * self.odd
        self.has_low = self.me >= 2
        self.has_high = self.me + 2 < size
        self.has_far = jnp.logical_and(self.far >= 0, self.far < size)

    def copy(self, src, slot, sem, target):
        return pltpu.make_async_remote_copy(
            src_ref=src,
            dst_ref=self.out.at[slot],
            send_sem=self.send.at[sem],
            recv_sem=self.recv.at[sem],
            device_id={"tm": target},
            device_id_type=MESH,
        )

    def up(self):
        return self.copy(self.x, 1, 0, self.me + 2)

    def down(self):
        return self.copy(self.x, 5, 1, self.me - 2)

    def across(self):
        return self.copy(self.x, 2 + 2 * self.odd, 2, self.sibling)

    def remote(self):
        return self.copy(self.x, 6 - 6 * self.odd, 3, self.far)

    def pass_low(self):
        return self.copy(self.out.at[1], 2 * self.odd, 4, self.sibling)

    def pass_high(self):
        return self.copy(self.out.at[5], 4 + 2 * self.odd, 5, self.sibling)

    def local(self):
        return pltpu.make_async_copy(self.x, self.out.at[3], self.send.at[6])

    def begin(self):
        barrier = pltpu.get_barrier_semaphore()

        def greet(target):
            pl.semaphore_signal(barrier, inc=1, device_id={"tm": target}, device_id_type=MESH)

        greet(self.sibling)
        pl.when(self.has_low)(lambda: greet(self.me - 2))
        pl.when(self.has_high)(lambda: greet(self.me + 2))
        pl.when(self.has_far)(lambda: greet(self.far))
        self.local().start()
        for slot in range(7):
            if slot != 3:
                other = self.me + slot - 3
                outside = jnp.logical_or(other < 0, other >= self.size)

                @pl.when(outside)
                def _(slot=slot):
                    self.out[slot] = jnp.zeros(self.out.shape[1:], self.out.dtype)

        peers = 1
        for has in (self.has_low, self.has_high, self.has_far):
            peers += jnp.where(has, 1, 0)
        pl.semaphore_wait(barrier, peers)
        pl.when(self.has_high)(lambda: self.up().start())
        pl.when(self.has_low)(lambda: self.down().start())
        pl.when(self.has_far)(lambda: self.remote().start())
        self.across().start()

    def forward(self):
        @pl.when(self.has_low)
        def _():
            self.up().wait_recv()
            self.pass_low().start()

        @pl.when(self.has_high)
        def _():
            self.down().wait_recv()
            self.pass_high().start()

    def finish(self):
        self.local().wait()
        self.across().wait()
        pl.when(self.has_far)(lambda: self.remote().wait())

        @pl.when(self.has_low)
        def _():
            self.down().wait_send()
            self.pass_low().wait()

        @pl.when(self.has_high)
        def _():
            self.up().wait_send()
            self.pass_high().wait()


EXCHANGE_SEMS = [pltpu.SemaphoreType.DMA((7,)), pltpu.SemaphoreType.DMA((6,))]


def subsample_kernel(
    size,
    x_ref,
    stem_ref,
    mid_dw_ref,
    mid_pw_ref,
    last_dw_ref,
    last_pw_ref,
    cot_ref,
    flat_ref,
    turned_ref,
    window_ref,
    even,
    odd,
    second,
    shifted,
    taps_ref,
    send,
    recv,
):
    exchange = Exchange(size, cot_ref, window_ref, send, recv)
    exchange.begin()
    rows = x_ref.shape[0] // 4
    main = rows - 8
    mids = second.shape[0] - 1
    span = shifted.shape[1] - 256
    odd[0] = jnp.zeros(odd.shape[1:], odd.dtype)
    second[0] = jnp.zeros(second.shape[1:], second.dtype)
    shifted[...] = jnp.zeros(shifted.shape, jnp.float32)
    for dt in range(3):
        for df in range(3):
            row = 3 * dt + df
            tap = stem_ref[dt, df : df + 1, :].astype(jnp.float32)
            for i in range(4):
                at = span + 2 * i + dt * MEL_PITCH + df
                shifted[i, at : at + 1, :] = tap
            taps_ref[row : row + 1, :] = mid_dw_ref[dt, df : df + 1, :].astype(jnp.float32)
            last = last_dw_ref[dt, df : df + 1, :].astype(jnp.float32)
            taps_ref[16 + row : 17 + row, :] = last

    def step(k, half):
        def stem(i):
            start = pl.multiple_of(span - 8 * k, 8)
            taps = shifted[i, pl.ds(start, 256), :].astype(jnp.bfloat16)
            return jnp.maximum(dot_nn(x_ref[...], taps), 0.0).reshape(even.shape)

        m = 2 * k + half
        even[...] = stem(2 * half)
        odd[1 - half] = stem(2 * half + 1)
        parts = (odd.at[half], even, odd.at[1 - half])
        early = jnp.zeros((main, 256), jnp.float32)
        late = jnp.zeros((rows, 256), jnp.float32)
        for df in range(3):
            src = parts[df]
            for dt in range(3):
                tap = taps_ref[3 * dt + df : 3 * dt + df + 1, :]
                phase = (3, 0, 1)[dt]
                start = 7 if dt == 0 else 8
                early += src[phase, start : start + main, :] * tap
                late += src[dt + 1] * tap
        weight = mid_pw_ref[...]
        second[m + 1, 0, 8:rows, :] = jnp.maximum(dot_nn(early.astype(jnp.bfloat16), weight), 0.0)
        second[m + 1, 1] = jnp.maximum(dot_nn(late.astype(jnp.bfloat16), weight), 0.0)

    def body(k, _):
        step(k, 0)
        step(k, 1)
        return 0

    lax.fori_loop(0, mids // 2, body, 0)
    exchange.forward()
    for f in range(mids // 2):
        total = jnp.zeros((main, 256), jnp.float32)
        for df in range(3):
            for dt in range(3):
                tap = taps_ref[16 + 3 * dt + df : 17 + 3 * dt + df, :]
                phase = (1, 0, 1)[dt]
                start = 7 if dt == 0 else 8
                total += second[2 * f + df, phase, start : start + main, :] * tap
        out = jnp.maximum(dot_nn(total.astype(jnp.bfloat16), last_pw_ref[...]), 0.0)
        flat_ref[:, f * 256 : (f + 1) * 256] = out.astype(jnp.bfloat16)
        turned_ref[f * 256 : (f + 1) * 256, :] = out.T.astype(jnp.bfloat16)
    exchange.finish()


def subsample(
    size,
    features,
    halo,
    stem_kernel,
    mid_depthwise,
    mid_pointwise,
    last_depthwise,
    last_pointwise,
    cotangent,
):
    feat_rows, mel = features.shape
    main = feat_rows // 8
    rows = main + 8
    channels = stem_kernel.shape[-1]
    mids = mel // 4
    blank = jnp.zeros((57, mel), features.dtype)
    series = jnp.concatenate([blank, halo, features, blank[:7]], axis=0)
    series = jnp.pad(series, ((0, 0), (1, MEL_PITCH - mel - 1)))
    eights = series.reshape(rows + 1, 8 * MEL_PITCH)
    wide = jnp.concatenate([eights[:-1], eights[1:, :MEL_PITCH]], axis=1)
    x = jnp.concatenate(
        [wide[:, 2 * p * MEL_PITCH : (2 * p + 3) * MEL_PITCH] for p in range(4)], axis=0
    )
    x = jnp.pad(x, ((0, 0), (0, 256 - 3 * MEL_PITCH)))
    return pl.pallas_call(
        functools.partial(subsample_kernel, size),
        out_shape=(
            jax.ShapeDtypeStruct((main, (mids // 2) * channels), jnp.bfloat16),
            jax.ShapeDtypeStruct(((mids // 2) * channels, main), jnp.bfloat16),
            jax.ShapeDtypeStruct((7,) + cotangent.shape, jnp.bfloat16),
        ),
        in_specs=[pl.BlockSpec(memory_space=pltpu.VMEM)] * 7,
        out_specs=(pl.BlockSpec(memory_space=pltpu.VMEM),) * 3,
        scratch_shapes=[
            pltpu.VMEM((4, rows, channels), jnp.float32),
            pltpu.VMEM((2, 4, rows, channels), jnp.float32),
            pltpu.VMEM((mids + 1, 2, rows, channels), jnp.float32),
            pltpu.VMEM((4, mel + 256, channels), jnp.float32),
            pltpu.VMEM((32, channels), jnp.float32),
        ]
        + EXCHANGE_SEMS,
        compiler_params=pltpu.CompilerParams(
            vmem_limit_bytes=40 * 1024 * 1024, collective_id=0, has_side_effects=True
        ),
        cost_estimate=pl.CostEstimate(
            flops=20_000_000_000, bytes_accessed=2_000_000, transcendentals=0
        ),
        name="subsample",
    )(
        x,
        stem_kernel,
        mid_depthwise,
        mid_pointwise,
        last_depthwise,
        last_pointwise,
        cotangent,
    )


def segments(positions, bounds_ref):
    found = jnp.zeros(positions.shape, jnp.int32)
    for u in range(bounds_ref.shape[0]):
        inside = (positions >= bounds_ref[u, 0]) & (positions < bounds_ref[u, 1])
        found = jnp.where(inside, u + 1, found)
    return found


PANEL = 256


class Half:
    def __init__(self, size):
        self.size, self.half = size, size // 2
        self.me = lax.axis_index("tm")
        self.base = self.me // self.half * self.half
        self.own = self.me - self.base
        self.partner = self.half - self.base + self.own
        self.core = lax.rem(self.me, 2)
        self.sibling = self.me + 1 - 2 * self.core
        self.across = self.me + 2 - 4 * lax.rem(self.me // 2, 2)
        self.steps = self.half // 4

    def turn(self, slot, step):
        return lax.rem(slot + 4 * step, self.half)

    def peer(self, distance):
        return self.base + lax.rem(self.own + distance, self.half)


def core_kernel(
    size,
    flat_ref,
    turned_ref,
    cot_ref,
    gain_ref,
    bounds_ref,
    live_ref,
    proj_hbm,
    qkv_hbm,
    out_hbm,
    block_out_ref,
    frame_grads_ref,
    proj_grads_ref,
    proj_w,
    qkv_w,
    out_w,
    xw,
    do_ref,
    pj,
    mixed_ref,
    grads_ref,
    bias_ref,
    stat_ref,
    normalized_ref,
    panels,
    columns,
    out_part,
    in_part,
    load_sem,
    send,
    recv,
    stat_send,
    stat_recv,
    col_send,
    col_recv,
    panel_send,
    panel_recv,
    part_send,
    part_recv,
):
    rows, width = block_out_ref.shape
    window = (2 * REACH + 1) * rows
    depth = flat_ref.shape[1]
    share = depth // size
    count = width // PANEL
    me = lax.axis_index("tm")
    half = Half(size)
    exchange = Exchange(size, xw.at[REACH], xw, send, recv)
    odd = exchange.odd
    offsets = [o for o in range(-REACH, REACH + 1) if o]

    piece = depth // 5
    loads = [
        pltpu.make_async_copy(
            proj_hbm.at[pl.ds(i * piece, piece), :],
            proj_w.at[pl.ds(i * piece, piece), :],
            load_sem.at[i],
        )
        for i in range(5)
    ]
    loads.append(pltpu.make_async_copy(out_hbm, out_w, load_sem.at[5]))
    loads.append(pltpu.make_async_copy(qkv_hbm, qkv_w, load_sem.at[6]))
    for load in loads:
        load.start()

    barrier = pltpu.get_barrier_semaphore()

    def greet(target):
        pl.semaphore_signal(barrier, inc=1, device_id={"tm": target}, device_id_type=MESH)

    for distance in range(1, size):
        greet(lax.rem(me + distance, size))

    def there(offset):
        return jnp.logical_and(me + offset >= 0, me + offset < size)

    def when_there(offset, action):
        pl.when(there(offset))(lambda: action(offset))

    for offset in offsets:

        @pl.when(jnp.logical_not(there(offset)))
        def _(offset=offset):
            xw[REACH + offset] = jnp.zeros(xw.shape[1:], xw.dtype)
            stat_ref[REACH + offset] = jnp.zeros(stat_ref.shape[1:], jnp.float32)

    total = jnp.zeros((rows, width), jnp.float32)
    for i in range(5):
        loads[i].wait()
        span = slice(i * piece, (i + 1) * piece)
        total += dot_nn(flat_ref[:, span], proj_w[span, :])
    frames = total.astype(jnp.bfloat16)
    frames_f = frames.astype(jnp.float32)
    centered = frames_f - jnp.mean(frames_f, axis=-1, keepdims=True)
    inv_std = lax.rsqrt(jnp.mean(centered * centered, axis=-1, keepdims=True) + norm_eps)
    normalized = centered * inv_std
    normalized_ref[...] = normalized
    block_out_ref[...] = frames
    xw[REACH] = (normalized * gain_ref[...]).astype(jnp.bfloat16)
    pl.semaphore_wait(barrier, size - 1)
    pl.when(exchange.has_high)(lambda: exchange.up().start())
    pl.when(exchange.has_low)(lambda: exchange.down().start())
    pl.when(exchange.has_far)(lambda: exchange.remote().start())
    exchange.across().start()

    loads[5].wait()
    cots = cot_ref[...].reshape(window, width)
    for i in range(0, width, 256):
        do_ref[:, i : i + 256] = dot_nt(cots, out_w[i : i + 256, :]).astype(jnp.bfloat16)

    first = (me - REACH) * rows
    own_col = segments(me * rows + lax.broadcasted_iota(jnp.int32, (rows, 128), 0), bounds_ref)
    for b in range(2 * REACH + 1):
        place = first + b * rows
        live = live_ref[0, b] == 1
        row = segments(place + lax.broadcasted_iota(jnp.int32, (8, rows), 1), bounds_ref)[0:1]
        same = (own_col[:, 0:1] == row) & live
        bias_ref[:, b * rows : (b + 1) * rows] = jnp.where(same, 0.0, neg_fill)

    loads[6].wait()

    def project(slot, blocks):
        x = xw[pl.ds(slot, blocks)].reshape(blocks * rows, width)
        for i in range(0, 3 * width, 512):
            out = dot_nn(x, qkv_w[:, i : i + 512]).astype(jnp.bfloat16)
            start = pl.multiple_of(slot * rows, rows)
            pj[pl.ds(start, blocks * rows), i : i + 512] = out

    exchange.across().wait_recv()
    project(REACH - odd, 2)
    exchange.forward()
    pl.when(exchange.has_low)(lambda: exchange.pass_low().wait_recv())
    project(1 - odd, 2)
    pl.when(exchange.has_high)(lambda: exchange.pass_high().wait_recv())
    project(5 - odd, 2)
    pl.when(exchange.has_far)(lambda: exchange.remote().wait_recv())
    project(6 * odd, 1)

    def turned(target):
        start = pl.multiple_of(target * share, 16)
        return turned_ref.at[pl.ds(start, share), :]

    def landing(which, slot):
        start = pl.multiple_of(slot * rows, rows)
        return columns.at[pl.ds(which * share, share), pl.ds(start, rows)]

    def column(which, distance):
        target = half.peer(distance)
        other = target if which == 0 else lax.rem(target + half.half, size)
        return pltpu.make_async_remote_copy(
            src_ref=turned(other),
            dst_ref=landing(which, half.own),
            send_sem=col_send.at[which, distance],
            recv_sem=col_recv.at[which, distance],
            device_id={"tm": target},
            device_id_type=MESH,
        )

    def column_in(which, distance):
        slot = lax.rem(half.own - distance + half.half, half.half)
        return pltpu.make_async_remote_copy(
            src_ref=turned(me),
            dst_ref=landing(which, slot),
            send_sem=col_send.at[which, distance],
            recv_sem=col_recv.at[which, distance],
            device_id={"tm": half.peer(distance)},
            device_id_type=MESH,
        )

    def column_own(which):
        other = me if which == 0 else half.partner
        return pltpu.make_async_copy(turned(other), landing(which, half.own), col_send.at[which, 0])

    for which in range(2):
        column_own(which).start()
        for distance in range(1, half.half):
            column(which, distance).start()

    own = slice(REACH * rows, (REACH + 1) * rows)
    lanes = lax.broadcasted_iota(jnp.int32, (rows, 128), 1)

    def head(group, h):
        return pl.ds(pl.multiple_of(group * width + h * HEAD_DIM, HEAD_DIM), HEAD_DIM)

    def forward(h, stats):
        keys = pj[:, head(1, h)]
        values = pj[:, head(2, h)]
        scores = dot_nt(pj[own, head(0, h)], keys) * SCALE + bias_ref[...]
        dprob = dot_nt(do_ref[own, head(0, h)], values)
        top = jnp.max(scores, axis=1, keepdims=True)
        weights = jnp.exp(scores - top)
        mass = jnp.sum(weights, axis=1, keepdims=True)
        probs = weights * (1.0 / mass)
        delta = jnp.sum(probs * dprob, axis=1, keepdims=True)
        dscore = (probs * (dprob - delta)).astype(jnp.bfloat16)
        mixed_ref[:, head(0, h)] = dot_nn(probs.astype(jnp.bfloat16), values).astype(jnp.bfloat16)
        grads_ref[:, head(0, h)] = (dot_nn(dscore, keys) * SCALE).astype(jnp.bfloat16)
        stats = jnp.where(lanes == h, top + jnp.log(mass), stats)
        return jnp.where(lanes == HEADS + h, delta, stats)

    stats = lax.fori_loop(0, HEADS, forward, jnp.zeros((rows, 128), jnp.float32))
    stat_ref[REACH] = stats.T[0 : 2 * HEADS, :]

    def stat_copy(offset, slot, sem):
        return pltpu.make_async_remote_copy(
            src_ref=stat_ref.at[REACH],
            dst_ref=stat_ref.at[slot],
            send_sem=stat_send.at[REACH + offset],
            recv_sem=stat_recv.at[sem],
            device_id={"tm": me + offset},
            device_id_type=MESH,
        )

    def stat_out(offset):
        return stat_copy(offset, REACH - offset, REACH - offset)

    def stat_in(offset):
        return stat_copy(offset, REACH + offset, REACH + offset)

    for offset in offsets:
        when_there(offset, lambda o: stat_out(o).start())
    block_out_ref[...] = (
        block_out_ref[...].astype(jnp.float32) + dot_nn(mixed_ref[...], out_w[...])
    ).astype(jnp.bfloat16)
    grad_normed = dot_nt(grads_ref[:, 0:width], qkv_w[:, 0:width])
    for offset in offsets:
        when_there(offset, lambda o: stat_in(o).wait_recv())

    def key_pass(h, _):
        queries = pj[:, head(0, h)]
        douts = do_ref[:, head(0, h)]
        blocks = range(2 * REACH + 1)
        log_norms = jnp.concatenate([stat_ref[b, pl.ds(h, 1), :] for b in blocks], axis=1)
        deltas = jnp.concatenate([stat_ref[b, pl.ds(HEADS + h, 1), :] for b in blocks], axis=1)
        scores = dot_nt(pj[own, head(1, h)], queries) * SCALE + bias_ref[...]
        dprob = dot_nt(pj[own, head(2, h)], douts)
        weights = jnp.exp(scores - log_norms)
        dscore = (weights * (dprob - deltas)).astype(jnp.bfloat16)
        grads_ref[:, head(1, h)] = (dot_nn(dscore, queries) * SCALE).astype(jnp.bfloat16)
        grads_ref[:, head(2, h)] = dot_nn(weights.astype(jnp.bfloat16), douts).astype(jnp.bfloat16)
        return 0

    lax.fori_loop(0, HEADS, key_pass, 0)
    grad_normed += dot_nt(grads_ref[:, width:], qkv_w[:, width:])
    normalized = normalized_ref[...]
    scaled = grad_normed * gain_ref[...]
    ln_grad = inv_std * (
        scaled
        - jnp.mean(scaled, axis=-1, keepdims=True)
        - normalized * jnp.mean(scaled * normalized, axis=-1, keepdims=True)
    )
    frame_grads = (cot_ref[REACH].astype(jnp.float32) + ln_grad).astype(jnp.bfloat16)
    for p in range(count):
        panels[p, half.own] = frame_grads[:, p * PANEL : (p + 1) * PANEL]

    def panel(p, slot, sem, target):
        return pltpu.make_async_remote_copy(
            src_ref=panels.at[p, slot],
            dst_ref=panels.at[p, slot],
            send_sem=panel_send.at[p, sem],
            recv_sem=panel_recv.at[p, sem],
            device_id={"tm": target},
            device_id_type=MESH,
        )

    steps = half.steps
    flip = half.across - half.me
    twin = half.sibling - half.me

    def along(p, s):
        return panel(p, half.own, s, half.base + half.turn(half.own, s))

    def along_in(p, s):
        return panel(p, half.turn(half.own, steps - s), s, half.base + half.turn(half.own, s))

    def cross(p, s):
        return panel(p, half.turn(half.own, steps - s), steps + s, half.across)

    def cross_in(p, s):
        return panel(p, half.turn(half.own, steps - s) + flip, steps + s, half.across)

    def twin_near(p, s):
        return panel(p, half.turn(half.own, steps - s), 2 * steps + s, half.sibling)

    def twin_near_in(p, s):
        return panel(p, half.turn(half.own, steps - s) + twin, 2 * steps + s, half.sibling)

    def twin_far(p, s):
        return panel(p, half.turn(half.own, steps - s) + flip, 3 * steps + s, half.sibling)

    def twin_far_in(p, s):
        return panel(p, half.turn(half.own, steps - s) + flip + twin, 3 * steps + s, half.sibling)

    def part(p):
        return pltpu.make_async_remote_copy(
            src_ref=out_part.at[p],
            dst_ref=in_part.at[p],
            send_sem=part_send.at[p],
            recv_sem=part_recv.at[p],
            device_id={"tm": half.partner},
            device_id_type=MESH,
        )

    for p in range(count):
        for s in range(1, steps):
            along(p, s).start()
        cross(p, 0).start()
        twin_near(p, 0).start()
    frame_grads_ref[...] = frame_grads
    for which in range(2):
        column_own(which).wait()
        for distance in range(1, half.half):
            column_in(which, distance).wait_recv()
    for p in range(count):
        for s in range(1, steps):
            along_in(p, s).wait_recv()
            cross(p, s).start()
            twin_near(p, s).start()
        for s in range(steps):
            cross_in(p, s).wait_recv()
            twin_far(p, s).start()
        for s in range(steps):
            twin_near_in(p, s).wait_recv()
            twin_far_in(p, s).wait_recv()
        sums = dot_nn(columns[...], panels[p].reshape(half.half * rows, PANEL))
        out_part[p] = sums[share:].astype(jnp.bfloat16)
        part(p).start()
        proj_grads_ref[:, p * PANEL : (p + 1) * PANEL] = sums[:share]
    for p in range(count):
        part(p).wait_recv()
        span = slice(p * PANEL, (p + 1) * PANEL)
        proj_grads_ref[:, span] = proj_grads_ref[:, span] + in_part[p].astype(jnp.float32)

    exchange.across().wait_send()
    pl.when(exchange.has_far)(lambda: exchange.remote().wait_send())

    @pl.when(exchange.has_low)
    def _():
        exchange.down().wait_send()
        exchange.pass_low().wait_send()

    @pl.when(exchange.has_high)
    def _():
        exchange.up().wait_send()
        exchange.pass_high().wait_send()

    for offset in offsets:
        when_there(offset, lambda o: stat_out(o).wait_send())
    for which in range(2):
        for distance in range(1, half.half):
            column(which, distance).wait_send()
    for p in range(count):
        for s in range(1, steps):
            along(p, s).wait_send()
        for s in range(steps):
            cross(p, s).wait_send()
            twin_near(p, s).wait_send()
            twin_far(p, s).wait_send()
        part(p).wait_send()


def core(
    size, flat, turned, cots, gain, bounds, live, proj_weight, qkv_weight, out_weight
):
    rows = flat.shape[0]
    depth, width = proj_weight.shape
    share = depth // size
    half = size // 2
    steps = half // 4
    count = width // PANEL
    blocks = 2 * REACH + 1
    vmem = pl.BlockSpec(memory_space=pltpu.VMEM)
    smem = pl.BlockSpec(memory_space=pltpu.SMEM)
    hbm = pl.BlockSpec(memory_space=pl.ANY)
    dma = pltpu.SemaphoreType.DMA
    bf16, f32 = jnp.bfloat16, jnp.float32
    return pl.pallas_call(
        functools.partial(core_kernel, size),
        out_shape=(
            jax.ShapeDtypeStruct((rows, width), bf16),
            jax.ShapeDtypeStruct((rows, width), bf16),
            jax.ShapeDtypeStruct((share, width), f32),
        ),
        in_specs=[vmem] * 4 + [smem] * 2 + [hbm] * 3,
        out_specs=(vmem,) * 3,
        scratch_shapes=[
            pltpu.VMEM(proj_weight.shape, bf16),
            pltpu.VMEM(qkv_weight.shape, bf16),
            pltpu.VMEM(out_weight.shape, bf16),
            pltpu.VMEM((blocks, rows, width), bf16),
            pltpu.VMEM((blocks * rows, width), bf16),
            pltpu.VMEM((blocks * rows, 3 * width), bf16),
            pltpu.VMEM((rows, width), bf16),
            pltpu.VMEM((rows, 3 * width), bf16),
            pltpu.VMEM((rows, blocks * rows), f32),
            pltpu.VMEM((blocks, 2 * HEADS, rows), f32),
            pltpu.VMEM((rows, width), f32),
            pltpu.VMEM((count, half, rows, PANEL), bf16),
            pltpu.VMEM((2 * share, half * rows), bf16),
            pltpu.VMEM((count, share, PANEL), bf16),
            pltpu.VMEM((count, share, PANEL), bf16),
            dma((7,)),
            dma((7,)),
            dma((6,)),
            dma((blocks,)),
            dma((blocks,)),
            dma((2, half)),
            dma((2, half)),
            dma((count, 4 * steps)),
            dma((count, 4 * steps)),
            dma((count,)),
            dma((count,)),
        ],
        compiler_params=pltpu.CompilerParams(
            vmem_limit_bytes=50 * 1024 * 1024, collective_id=1, has_side_effects=True
        ),
        name="core",
    )(flat, turned, cots, gain, bounds, live, proj_weight, qkv_weight, out_weight)


def per_device(
    size,
    features,
    stem_kernel,
    mid_depthwise,
    mid_pointwise,
    last_depthwise,
    last_pointwise,
    proj_weight,
    norm_gain,
    qkv_weight,
    out_weight,
    cotangent,
    utt_bounds,
    live_blocks,
):
    halo = lax.ppermute(features[-8:], "tm", [(i, i + 1) for i in range(size - 1)])
    flat, turned, cots = subsample(
        size,
        features,
        halo,
        stem_kernel,
        mid_depthwise,
        mid_pointwise,
        last_depthwise,
        last_pointwise,
        cotangent,
    )
    return core(
        size,
        flat,
        turned,
        cots,
        norm_gain.reshape(1, -1),
        utt_bounds,
        live_blocks,
        proj_weight,
        qkv_weight,
        out_weight,
    )


def solution(mesh):
    split = P(("groups", "tm"), None)
    in_specs = (split,) + (P(),) * 9 + (split, P("groups", None), split)
    return jax.shard_map(
        functools.partial(per_device, mesh.shape["tm"]),
        mesh=mesh,
        in_specs=in_specs,
        out_specs=(split, split, split),
        check_vma=False,
    )
```

```python
import functools

import jax
import jax.numpy as jnp
from jax import lax
from jax.experimental import pallas as pl
from jax.experimental.pallas import tpu as pltpu
from jax.sharding import PartitionSpec as P

HEADS = 8
REACH = 3
HEAD_DIM = 128
norm_eps = 1e-05
neg_fill = -1e30
MEL_PITCH = 84
SCALE = HEAD_DIM ** (-0.5)
PIECES = 4
PANEL = 128
AHEAD = 2


def dot_nt(a, b):
    return lax.dot_general(a, b, (((1,), (1,)), ((), ())), preferred_element_type=jnp.float32)


def dot_tn(a, b):
    return lax.dot_general(a, b, (((0,), (0,)), ((), ())), preferred_element_type=jnp.float32)


def dot_nn(a, b):
    return jnp.dot(a, b, preferred_element_type=jnp.float32)


MESH = pl.DeviceIdType.MESH


class Exchange:
    def __init__(self, size, out_ref, send, recv):
        self.size, self.out, self.send, self.recv = size, out_ref, send, recv
        self.rows = out_ref.shape[1] // PIECES
        self.me = lax.axis_index("tm")
        self.odd = lax.rem(self.me, 2)
        self.upper = lax.rem(self.me // 2, 2)
        self.sibling = self.me + 1 - 2 * self.odd
        self.beside = self.me + 2 - 4 * self.upper
        self.far = self.me - 3 + 6 * self.odd
        self.onward = self.me + 4 - 8 * self.upper
        self.back = self.me - 4 + 8 * self.upper
        self.has_far = self.inside(self.far)
        self.has_onward = self.inside(self.onward)
        self.has_back = self.inside(self.back)
        self.low = 1 + 4 * self.upper
        self.high = 5 - 4 * self.upper

    def inside(self, target):
        return jnp.logical_and(target >= 0, target < self.size)

    def copy(self, source, slot, sem, target):
        return pltpu.make_async_remote_copy(
            src_ref=self.out.at[source],
            dst_ref=self.out.at[slot],
            send_sem=self.send.at[sem],
            recv_sem=self.recv.at[sem],
            device_id={"tm": target},
            device_id_type=MESH,
        )

    def piece(self, source, slot, sem, target, j):
        span = pl.ds(j * self.rows, self.rows)
        return pltpu.make_async_remote_copy(
            src_ref=self.out.at[source, span, :],
            dst_ref=self.out.at[slot, span, :],
            send_sem=self.send.at[sem],
            recv_sem=self.recv.at[sem],
            device_id={"tm": target},
            device_id_type=MESH,
        )

    def twin(self):
        return self.copy(REACH, 2 + 2 * self.odd, 0, self.sibling)

    def remote(self):
        return self.copy(REACH, 6 - 6 * self.odd, 1, self.far)

    def near(self, j):
        return self.piece(REACH, self.low, 2 + j, self.beside, j)

    def near_in(self, j):
        return self.piece(REACH, self.high, 2 + j, self.beside, j)

    def deep(self, j):
        return self.piece(self.high, self.low, 2 + PIECES + j, self.onward, j)

    def deep_in(self, j):
        return self.piece(REACH, self.low, 2 + PIECES + j, self.back, j)

    def near_pass(self, j):
        slot = 4 - 4 * self.upper + 2 * self.odd
        return self.piece(self.high, slot, 2 + 2 * PIECES + j, self.sibling, j)

    def near_pass_in(self, j):
        slot = 6 - 4 * self.upper - 2 * self.odd
        return self.piece(REACH, slot, 2 + 2 * PIECES + j, self.sibling, j)

    def deep_pass(self, j):
        slot = 4 * self.upper + 2 * self.odd
        return self.piece(self.low, slot, 2 + 3 * PIECES + j, self.sibling, j)

    def deep_pass_in(self, j):
        slot = 4 * self.upper + 2 - 2 * self.odd
        return self.piece(REACH, slot, 2 + 3 * PIECES + j, self.sibling, j)

    def blank(self):
        for slot in range(2 * REACH + 1):
            if slot != REACH:

                @pl.when(jnp.logical_not(self.inside(self.me + slot - REACH)))
                def _(slot=slot):
                    self.out[slot] = jnp.zeros(self.out.shape[1:], self.out.dtype)

    def start(self):
        for j in range(PIECES):
            self.near(j).start()
        pl.when(self.has_far)(lambda: self.remote().start())
        self.twin().start()

    def relay(self, j):
        self.near_in(j).wait_recv()
        pl.when(self.has_onward)(lambda: self.deep(j).start())
        self.near_pass(j).start()

    def relay_deep(self, j):
        @pl.when(self.has_back)
        def _():
            self.deep_in(j).wait_recv()
            self.deep_pass(j).start()

    def near_done(self):
        for j in range(PIECES):
            self.near_pass_in(j).wait_recv()

    def deep_done(self):
        for j in range(PIECES):
            pl.when(self.has_back)(lambda: self.deep_pass_in(j).wait_recv())

    def drain(self):
        self.twin().wait_send()
        pl.when(self.has_far)(lambda: self.remote().wait_send())
        for j in range(PIECES):
            self.near(j).wait_send()
            self.near_pass(j).wait_send()
            pl.when(self.has_onward)(lambda: self.deep(j).wait_send())
            pl.when(self.has_back)(lambda: self.deep_pass(j).wait_send())


def segments(positions, bounds_ref):
    found = jnp.zeros(positions.shape, jnp.int32)
    for u in range(bounds_ref.shape[1]):
        inside = (positions >= bounds_ref[0, u]) & (positions < bounds_ref[1, u])
        found = jnp.where(inside, u + 1, found)
    return found


class Subsample:
    def __init__(self, x, stem_w, mid_dw, mid_w, last_dw, last_w, flat, turned, even, odd, second, shifted, taps):
        self.x, self.stem_w, self.mid_dw, self.mid_w = x, stem_w, mid_dw, mid_w
        self.last_dw, self.last_w, self.flat, self.turned = last_dw, last_w, flat, turned
        self.even, self.odd, self.second, self.shifted, self.taps = even, odd, second, shifted, taps
        self.rows = x.shape[0] // 4
        self.main = self.rows - 8
        self.mids = second.shape[0] - 1
        self.span = shifted.shape[1] - 256

    def blank(self):
        self.odd[0] = jnp.zeros(self.odd.shape[1:], self.odd.dtype)
        self.second[0] = jnp.zeros(self.second.shape[1:], self.second.dtype)
        self.shifted[...] = jnp.zeros(self.shifted.shape, jnp.float32)

    def spread(self):
        for dt in range(3):
            for df in range(3):
                row = 3 * dt + df
                tap = self.stem_w[dt, df : df + 1, :].astype(jnp.float32)
                for i in range(4):
                    at = self.span + 2 * i + dt * MEL_PITCH + df
                    self.shifted[i, at : at + 1, :] = tap
                self.taps[row : row + 1, :] = self.mid_dw[dt, df : df + 1, :].astype(jnp.float32)
                last = self.last_dw[dt, df : df + 1, :].astype(jnp.float32)
                self.taps[16 + row : 17 + row, :] = last

    def step(self, k, half):
        main, rows, second = self.main, self.rows, self.second

        def stem(i):
            start = pl.multiple_of(self.span - 8 * k, 8)
            taps = self.shifted[i, pl.ds(start, 256), :].astype(jnp.bfloat16)
            return jnp.maximum(dot_nn(self.x[...], taps), 0.0).reshape(self.even.shape)

        m = 2 * k + half
        self.even[...] = stem(2 * half)
        self.odd[1 - half] = stem(2 * half + 1)
        parts = (self.odd.at[half], self.even, self.odd.at[1 - half])
        early = jnp.zeros((main, 256), jnp.float32)
        late = jnp.zeros((rows, 256), jnp.float32)
        for df in range(3):
            part = parts[df]
            for dt in range(3):
                tap = self.taps[3 * dt + df : 3 * dt + df + 1, :]
                phase = (3, 0, 1)[dt]
                start = 7 if dt == 0 else 8
                early += part[phase, start : start + main, :] * tap
                late += part[dt + 1] * tap
        weight = self.mid_w[...]
        second[m + 1, 0, 8:rows, :] = jnp.maximum(dot_nn(early.astype(jnp.bfloat16), weight), 0.0)
        second[m + 1, 1] = jnp.maximum(dot_nn(late.astype(jnp.bfloat16), weight), 0.0)

    def run(self, first, last):
        def body(k, _):
            self.step(k, 0)
            self.step(k, 1)
            return 0

        lax.fori_loop(first, last, body, 0)

    def finish(self, f):
        total = jnp.zeros((self.main, 256), jnp.float32)
        for df in range(3):
            for dt in range(3):
                tap = self.taps[16 + 3 * dt + df : 17 + 3 * dt + df, :]
                phase = (1, 0, 1)[dt]
                start = 7 if dt == 0 else 8
                total += self.second[2 * f + df, phase, start : start + self.main, :] * tap
        out = jnp.maximum(dot_nn(total.astype(jnp.bfloat16), self.last_w[...]), 0.0)
        self.flat[:, f * 256 : (f + 1) * 256] = out.astype(jnp.bfloat16)
        self.turned[f * 256 : (f + 1) * 256, :] = out.T.astype(jnp.bfloat16)


class Half:
    def __init__(self, size):
        self.size, self.half = size, size // 2
        self.me = lax.axis_index("tm")
        self.base = self.me // self.half * self.half
        self.own = self.me - self.base
        self.partner = self.half - self.base + self.own
        self.core = lax.rem(self.me, 2)
        self.sibling = self.me + 1 - 2 * self.core
        self.across = self.me + 2 - 4 * lax.rem(self.me // 2, 2)
        self.steps = self.half // 4

    def turn(self, slot, step):
        return lax.rem(slot + 4 * step, self.half)

    def peer(self, distance):
        return self.base + lax.rem(self.own + distance, self.half)


def core_kernel(
    size,
    x_ref,
    gain_ref,
    bounds_ref,
    live_ref,
    stem_hbm,
    mid_dw_hbm,
    mid_w_hbm,
    last_dw_hbm,
    last_w_hbm,
    cot_hbm,
    proj_hbm,
    qkv_hbm,
    out_hbm,
    block_out_ref,
    frame_grads_ref,
    proj_grads_ref,
    stem_w,
    mid_dw,
    mid_w,
    last_dw,
    last_w,
    x_own,
    halo_out,
    halo_in,
    flat_ref,
    turned_ref,
    even,
    odd_part,
    second,
    shifted,
    taps,
    cot_ref,
    proj_w,
    qkv_w,
    out_w,
    xw,
    do_ref,
    pj,
    mixed_ref,
    grads_ref,
    bias_ref,
    stat_ref,
    normalized_ref,
    panels,
    columns,
    out_part,
    in_part,
    load_sem,
    halo_sem,
    cot_send,
    cot_recv,
    send,
    recv,
    stat_send,
    stat_recv,
    col_send,
    col_recv,
    panel_send,
    panel_recv,
    part_send,
    part_recv,
):
    rows, width = block_out_ref.shape
    window = (2 * REACH + 1) * rows
    depth = flat_ref.shape[1]
    share = depth // size
    count = width // PANEL
    me = lax.axis_index("tm")
    half = Half(size)
    cot_exchange = Exchange(size, cot_ref, cot_send, cot_recv)
    exchange = Exchange(size, xw, send, recv)
    odd = exchange.odd
    offsets = [o for o in range(-REACH, REACH + 1) if o]
    conv = Subsample(
        x_own, stem_w, mid_dw, mid_w, last_dw, last_w, flat_ref, turned_ref, even, odd_part, second, shifted, taps
    )

    def load(i, source, target):
        return pltpu.make_async_copy(source, target, load_sem.at[i])

    small = [
        load(0, cot_hbm, cot_ref.at[REACH]),
        load(1, stem_hbm, stem_w),
        load(2, mid_dw_hbm, mid_dw),
        load(3, mid_w_hbm, mid_w),
        load(4, last_dw_hbm, last_dw),
        load(5, last_w_hbm, last_w),
    ]
    large = [load(6, proj_hbm, proj_w), load(7, out_hbm, out_w), load(8, qkv_hbm, qkv_w)]
    for item in small:
        item.start()

    barrier = pltpu.get_barrier_semaphore()
    peers = 0
    for distance in range(1, size):
        other = lax.rem(me + distance, size)
        gap = other - me
        near = jnp.logical_and(gap >= -4, gap <= 4)
        same = other // half.half == me // half.half
        known = jnp.logical_or(jnp.logical_or(near, same), other == half.partner)
        peers += jnp.where(known, 1, 0)

        @pl.when(known)
        def _(other=other):
            pl.semaphore_signal(barrier, inc=1, device_id={"tm": other}, device_id_type=MESH)

    def there(offset):
        return jnp.logical_and(me + offset >= 0, me + offset < size)

    def when_there(offset, action):
        pl.when(there(offset))(lambda: action(offset))

    for offset in offsets:

        @pl.when(jnp.logical_not(there(offset)))
        def _(offset=offset):
            stat_ref[REACH + offset] = jnp.zeros(stat_ref.shape[1:], jnp.float32)

    slab = conv.rows
    tails = [x_ref[p * slab + slab - 16 : p * slab + slab, :].astype(jnp.float32)[8:16] for p in range(4)]
    for p in range(4):
        halo_out[8 * p : 8 * p + 8, :] = tails[p]
    halo_out[32:40, :] = pltpu.roll(tails[3], 256 - 2 * MEL_PITCH, 1)

    @pl.when(me == 0)
    def _():
        halo_in[...] = jnp.zeros(halo_in.shape, jnp.float32)

    def halo(target):
        return pltpu.make_async_remote_copy(
            src_ref=halo_out,
            dst_ref=halo_in,
            send_sem=halo_sem.at[0],
            recv_sem=halo_sem.at[1],
            device_id={"tm": target},
            device_id_type=MESH,
        )

    conv.blank()
    x_own[...] = x_ref[...]
    small[0].wait()
    pl.semaphore_wait(barrier, peers)
    pl.when(me + 1 < size)(lambda: halo(me + 1).start())
    cot_exchange.start()
    for item in large:
        item.start()
    for item in small[1:]:
        item.wait()
    conv.spread()
    cot_exchange.blank()
    exchange.blank()
    pl.when(me > 0)(lambda: halo(me - 1).wait_recv())
    place = lax.broadcasted_iota(jnp.int32, (8, 256), 0)
    lane = lax.broadcasted_iota(jnp.int32, (8, 256), 1)
    for p in range(4):
        top = x_own[p * slab : p * slab + 16, :].astype(jnp.float32)
        upper = jnp.where(place == 7, halo_in[8 * p : 8 * p + 8, :], top[0:8])
        lower = top[8:16]
        if p == 0:
            carried = jnp.broadcast_to(halo_in[39:40, :], (8, 256))
            lower = jnp.where((place == 0) & (lane < MEL_PITCH), carried, lower)
        x_own[p * slab : p * slab + 16, :] = jnp.concatenate([upper, lower], axis=0).astype(jnp.bfloat16)

    turns = conv.mids // 2
    cut = [turns * i // 6 for i in range(7)]
    conv.run(cut[0], cut[2])
    cot_exchange.relay(0)
    conv.run(cut[2], cut[3])
    cot_exchange.relay(1)
    conv.run(cut[3], cut[4])
    cot_exchange.relay(2)
    conv.run(cut[4], cut[5])
    cot_exchange.relay(3)
    cot_exchange.relay_deep(0)
    conv.run(cut[5], cut[6])
    for j in range(1, PIECES):
        cot_exchange.relay_deep(j)
    for f in range(turns):
        conv.finish(f)

    large[0].wait()
    frames = dot_nn(flat_ref[...], proj_w[...]).astype(jnp.bfloat16)
    frames_f = frames.astype(jnp.float32)
    centered = frames_f - jnp.mean(frames_f, axis=-1, keepdims=True)
    inv_std = lax.rsqrt(jnp.mean(centered * centered, axis=-1, keepdims=True) + norm_eps)
    normalized = centered * inv_std
    normalized_ref[...] = normalized
    block_out_ref[...] = frames
    xw[REACH] = (normalized * gain_ref[...]).astype(jnp.bfloat16)
    exchange.start()
    large[1].wait()
    cot_exchange.near_done()
    cot_exchange.deep_done()
    cot_exchange.twin().wait_recv()
    pl.when(cot_exchange.has_far)(lambda: cot_exchange.remote().wait_recv())
    cots = cot_ref[...].reshape(window, width)

    def d_attention(first, last):
        for i in range(first, last, 256):
            do_ref[:, i : i + 256] = dot_nt(cots, out_w[i : i + 256, :]).astype(jnp.bfloat16)

    first = (me - REACH) * rows
    own_col = segments(me * rows + lax.broadcasted_iota(jnp.int32, (rows, 128), 0), bounds_ref)
    for b in range(2 * REACH + 1):
        place = first + b * rows
        live = live_ref[0, b] == 1
        row = segments(place + lax.broadcasted_iota(jnp.int32, (8, rows), 1), bounds_ref)[0:1]
        same = (own_col[:, 0:1] == row) & live
        bias_ref[:, b * rows : (b + 1) * rows] = jnp.where(same, 0.0, neg_fill)

    large[2].wait()

    def project(slot, blocks, first, last):
        x = xw[pl.ds(slot, blocks)].reshape(blocks * rows, width)
        for i in range(first, last, 512):
            out = dot_nn(x, qkv_w[:, i : i + 512]).astype(jnp.bfloat16)
            start = pl.multiple_of(slot * rows, rows)
            pj[pl.ds(start, blocks * rows), i : i + 512] = out

    d_attention(0, width // 2)
    exchange.relay(0)
    exchange.twin().wait_recv()
    project(REACH - odd, 2, 0, 3 * width // 2)
    exchange.relay(1)
    project(REACH - odd, 2, 3 * width // 2, 3 * width)
    exchange.relay(2)
    exchange.relay_deep(0)
    d_attention(width // 2, width)
    exchange.relay(3)
    exchange.relay_deep(1)
    near_slot = (1 - odd) * exchange.upper + (5 - odd) * (1 - exchange.upper)
    deep_slot = (5 - odd) * exchange.upper + (1 - odd) * (1 - exchange.upper)
    pl.when(exchange.has_far)(lambda: exchange.remote().wait_recv())
    project(6 * odd, 1, 0, 3 * width)
    exchange.near_done()
    exchange.relay_deep(2)
    project(near_slot, 2, 0, 3 * width // 2)
    exchange.relay_deep(3)
    project(near_slot, 2, 3 * width // 2, 3 * width)
    exchange.deep_done()
    project(deep_slot, 2, 0, 3 * width)

    def turned(target):
        start = pl.multiple_of(target * share, 16)
        return turned_ref.at[pl.ds(start, share), :]

    def landing(which, slot):
        start = pl.multiple_of(slot * rows, rows)
        return columns.at[pl.ds(which * share, share), pl.ds(start, rows)]

    def column(which, distance):
        target = half.peer(distance)
        other = target if which == 0 else lax.rem(target + half.half, size)
        return pltpu.make_async_remote_copy(
            src_ref=turned(other),
            dst_ref=landing(which, half.own),
            send_sem=col_send.at[which, distance],
            recv_sem=col_recv.at[which, distance],
            device_id={"tm": target},
            device_id_type=MESH,
        )

    def column_in(which, distance):
        slot = lax.rem(half.own - distance + half.half, half.half)
        return pltpu.make_async_remote_copy(
            src_ref=turned(me),
            dst_ref=landing(which, slot),
            send_sem=col_send.at[which, distance],
            recv_sem=col_recv.at[which, distance],
            device_id={"tm": half.peer(distance)},
            device_id_type=MESH,
        )

    def column_own(which):
        other = me if which == 0 else half.partner
        return pltpu.make_async_copy(turned(other), landing(which, half.own), col_send.at[which, 0])

    for which in range(2):
        column_own(which).start()
        for distance in range(1, half.half):
            column(which, distance).start()

    own = slice(REACH * rows, (REACH + 1) * rows)
    lanes = lax.broadcasted_iota(jnp.int32, (rows, 128), 1)

    def head(group, h):
        return pl.ds(pl.multiple_of(group * width + h * HEAD_DIM, HEAD_DIM), HEAD_DIM)

    def forward(h, stats):
        keys = pj[:, head(1, h)]
        values = pj[:, head(2, h)]
        scores = dot_nt(pj[own, head(0, h)], keys) * SCALE + bias_ref[...]
        dprob = dot_nt(do_ref[own, head(0, h)], values)
        top = jnp.max(scores, axis=1, keepdims=True)
        weights = jnp.exp(scores - top)
        mass = jnp.sum(weights, axis=1, keepdims=True)
        probs = weights * (1.0 / mass)
        delta = jnp.sum(probs * dprob, axis=1, keepdims=True)
        dscore = (probs * (dprob - delta)).astype(jnp.bfloat16)
        mixed_ref[:, head(0, h)] = dot_nn(probs.astype(jnp.bfloat16), values).astype(jnp.bfloat16)
        grads_ref[:, head(0, h)] = (dot_nn(dscore, keys) * SCALE).astype(jnp.bfloat16)
        stats = jnp.where(lanes == h, top + jnp.log(mass), stats)
        return jnp.where(lanes == HEADS + h, delta, stats)

    stats = lax.fori_loop(0, HEADS, forward, jnp.zeros((rows, 128), jnp.float32))
    stat_ref[REACH] = stats.T[0 : 2 * HEADS, :]

    def stat_copy(offset, slot, sem):
        return pltpu.make_async_remote_copy(
            src_ref=stat_ref.at[REACH],
            dst_ref=stat_ref.at[slot],
            send_sem=stat_send.at[REACH + offset],
            recv_sem=stat_recv.at[sem],
            device_id={"tm": me + offset},
            device_id_type=MESH,
        )

    def stat_out(offset):
        return stat_copy(offset, REACH - offset, REACH - offset)

    def stat_in(offset):
        return stat_copy(offset, REACH + offset, REACH + offset)

    for offset in offsets:
        when_there(offset, lambda o: stat_out(o).start())
    block_out_ref[...] = (
        block_out_ref[...].astype(jnp.float32) + dot_nn(mixed_ref[...], out_w[...])
    ).astype(jnp.bfloat16)
    grad_normed = dot_nt(grads_ref[:, 0:width], qkv_w[:, 0:width])
    for offset in offsets:
        when_there(offset, lambda o: stat_in(o).wait_recv())

    def key_pass(h, _):
        queries = pj[:, head(0, h)]
        douts = do_ref[:, head(0, h)]
        blocks = range(2 * REACH + 1)
        log_norms = jnp.concatenate([stat_ref[b, pl.ds(h, 1), :] for b in blocks], axis=1)
        deltas = jnp.concatenate([stat_ref[b, pl.ds(HEADS + h, 1), :] for b in blocks], axis=1)
        scores = dot_nt(pj[own, head(1, h)], queries) * SCALE + bias_ref[...]
        dprob = dot_nt(pj[own, head(2, h)], douts)
        weights = jnp.exp(scores - log_norms)
        dscore = (weights * (dprob - deltas)).astype(jnp.bfloat16)
        grads_ref[:, head(1, h)] = (dot_nn(dscore, queries) * SCALE).astype(jnp.bfloat16)
        grads_ref[:, head(2, h)] = dot_nn(weights.astype(jnp.bfloat16), douts).astype(jnp.bfloat16)
        return 0

    lax.fori_loop(0, HEADS, key_pass, 0)
    grad_normed += dot_nt(grads_ref[:, width:], qkv_w[:, width:])
    normalized = normalized_ref[...]
    scaled = grad_normed * gain_ref[...]
    ln_grad = inv_std * (
        scaled
        - jnp.mean(scaled, axis=-1, keepdims=True)
        - normalized * jnp.mean(scaled * normalized, axis=-1, keepdims=True)
    )
    frame_grads = (cot_ref[REACH].astype(jnp.float32) + ln_grad).astype(jnp.bfloat16)
    for p in range(count):
        panels[p, half.own] = frame_grads[:, p * PANEL : (p + 1) * PANEL]

    def panel(p, slot, sem, target):
        return pltpu.make_async_remote_copy(
            src_ref=panels.at[p, slot],
            dst_ref=panels.at[p, slot],
            send_sem=panel_send.at[p, sem],
            recv_sem=panel_recv.at[p, sem],
            device_id={"tm": target},
            device_id_type=MESH,
        )

    steps = half.steps
    flip = half.across - half.me
    twin = half.sibling - half.me

    def along(p, s):
        return panel(p, half.own, s, half.base + half.turn(half.own, s))

    def along_in(p, s):
        return panel(p, half.turn(half.own, steps - s), s, half.base + half.turn(half.own, s))

    def cross(p, s):
        return panel(p, half.turn(half.own, steps - s), steps + s, half.across)

    def cross_in(p, s):
        return panel(p, half.turn(half.own, steps - s) + flip, steps + s, half.across)

    def twin_near(p, s):
        return panel(p, half.turn(half.own, steps - s), 2 * steps + s, half.sibling)

    def twin_near_in(p, s):
        return panel(p, half.turn(half.own, steps - s) + twin, 2 * steps + s, half.sibling)

    def twin_far(p, s):
        return panel(p, half.turn(half.own, steps - s) + flip, 3 * steps + s, half.sibling)

    def twin_far_in(p, s):
        return panel(p, half.turn(half.own, steps - s) + flip + twin, 3 * steps + s, half.sibling)

    def part(p):
        return pltpu.make_async_remote_copy(
            src_ref=out_part.at[p],
            dst_ref=in_part.at[p],
            send_sem=part_send.at[p],
            recv_sem=part_recv.at[p],
            device_id={"tm": half.partner},
            device_id_type=MESH,
        )

    def relay(p):
        for s in range(1, steps):
            along_in(p, s).wait_recv()
            cross(p, s).start()
            twin_near(p, s).start()

    def share_far(p):
        for s in range(steps):
            cross_in(p, s).wait_recv()
            twin_far(p, s).start()

    def multiply(p):
        for s in range(steps):
            twin_near_in(p, s).wait_recv()
            twin_far_in(p, s).wait_recv()
        sums = dot_nn(columns[...], panels[p].reshape(half.half * rows, PANEL))
        out_part[p] = sums[share:].astype(jnp.bfloat16)
        part(p).start()
        proj_grads_ref[:, p * PANEL : (p + 1) * PANEL] = sums[:share]

    for p in range(count):
        for s in range(1, steps):
            along(p, s).start()
        if p < AHEAD:
            cross(p, 0).start()
        twin_near(p, 0).start()
    frame_grads_ref[...] = frame_grads
    for which in range(2):
        column_own(which).wait()
        for distance in range(1, half.half):
            column_in(which, distance).wait_recv()
    for t in range(count + 2):
        if t < count:
            relay(t)
            if t + AHEAD < count:
                cross(t + AHEAD, 0).start()
        if 1 <= t <= count:
            share_far(t - 1)
        if t >= 2:
            multiply(t - 2)
    for p in range(count):
        part(p).wait_recv()
        span = slice(p * PANEL, (p + 1) * PANEL)
        proj_grads_ref[:, span] = proj_grads_ref[:, span] + in_part[p].astype(jnp.float32)

    cot_exchange.drain()
    exchange.drain()
    pl.when(me + 1 < size)(lambda: halo(me + 1).wait_send())
    for offset in offsets:
        when_there(offset, lambda o: stat_out(o).wait_send())
    for which in range(2):
        for distance in range(1, half.half):
            column(which, distance).wait_send()
    for p in range(count):
        for s in range(1, steps):
            along(p, s).wait_send()
        for s in range(steps):
            cross(p, s).wait_send()
            twin_near(p, s).wait_send()
            twin_far(p, s).wait_send()
        part(p).wait_send()


def arranged(features):
    feat_rows, mel = features.shape
    rows = feat_rows // 8 + 8
    series = jnp.pad(features, ((65, 7), (1, MEL_PITCH - mel - 1)))
    eights = series.reshape(rows + 1, 8 * MEL_PITCH)
    wide = jnp.concatenate([eights[:-1], eights[1:, :MEL_PITCH]], axis=1)
    x = jnp.concatenate(
        [wide[:, 2 * p * MEL_PITCH : (2 * p + 3) * MEL_PITCH] for p in range(4)], axis=0
    )
    return jnp.pad(x, ((0, 0), (0, 256 - 3 * MEL_PITCH)))


def core(
    size,
    mel,
    x,
    gain,
    bounds,
    live,
    stem_kernel,
    mid_depthwise,
    mid_pointwise,
    last_depthwise,
    last_pointwise,
    cotangent,
    proj_weight,
    qkv_weight,
    out_weight,
):
    rows = cotangent.shape[0]
    slab = rows + 8
    mids = mel // 4
    channels = stem_kernel.shape[-1]
    depth, width = proj_weight.shape
    share = depth // size
    half = size // 2
    steps = half // 4
    count = width // PANEL
    blocks = 2 * REACH + 1
    vmem = pl.BlockSpec(memory_space=pltpu.VMEM)
    smem = pl.BlockSpec(memory_space=pltpu.SMEM)
    hbm = pl.BlockSpec(memory_space=pltpu.HBM)
    dma = pltpu.SemaphoreType.DMA
    bf16, f32 = jnp.bfloat16, jnp.float32
    return pl.pallas_call(
        functools.partial(core_kernel, size),
        out_shape=(
            jax.ShapeDtypeStruct((rows, width), bf16),
            jax.ShapeDtypeStruct((rows, width), bf16),
            jax.ShapeDtypeStruct((share, width), f32),
        ),
        in_specs=[vmem] * 2 + [smem] * 2 + [hbm] * 9,
        out_specs=(vmem,) * 3,
        scratch_shapes=[
            pltpu.VMEM(stem_kernel.shape, bf16),
            pltpu.VMEM(mid_depthwise.shape, bf16),
            pltpu.VMEM(mid_pointwise.shape, bf16),
            pltpu.VMEM(last_depthwise.shape, bf16),
            pltpu.VMEM(last_pointwise.shape, bf16),
            pltpu.VMEM(x.shape, bf16),
            pltpu.VMEM((40, 256), f32),
            pltpu.VMEM((40, 256), f32),
            pltpu.VMEM((rows, depth), bf16),
            pltpu.VMEM((depth, rows), bf16),
            pltpu.VMEM((4, slab, channels), f32),
            pltpu.VMEM((2, 4, slab, channels), f32),
            pltpu.VMEM((mids + 1, 2, slab, channels), f32),
            pltpu.VMEM((4, mel + 256, channels), f32),
            pltpu.VMEM((32, channels), f32),
            pltpu.VMEM((blocks, rows, width), bf16),
            pltpu.VMEM(proj_weight.shape, bf16),
            pltpu.VMEM(qkv_weight.shape, bf16),
            pltpu.VMEM(out_weight.shape, bf16),
            pltpu.VMEM((blocks, rows, width), bf16),
            pltpu.VMEM((blocks * rows, width), bf16),
            pltpu.VMEM((blocks * rows, 3 * width), bf16),
            pltpu.VMEM((rows, width), bf16),
            pltpu.VMEM((rows, 3 * width), bf16),
            pltpu.VMEM((rows, blocks * rows), f32),
            pltpu.VMEM((blocks, 2 * HEADS, rows), f32),
            pltpu.VMEM((rows, width), f32),
            pltpu.VMEM((count, half, rows, PANEL), bf16),
            pltpu.VMEM((2 * share, half * rows), bf16),
            pltpu.VMEM((count, share, PANEL), bf16),
            pltpu.VMEM((count, share, PANEL), bf16),
            dma((9,)),
            dma((2,)),
            dma((2 + 4 * PIECES,)),
            dma((2 + 4 * PIECES,)),
            dma((2 + 4 * PIECES,)),
            dma((2 + 4 * PIECES,)),
            dma((blocks,)),
            dma((blocks,)),
            dma((2, half)),
            dma((2, half)),
            dma((count, 4 * steps)),
            dma((count, 4 * steps)),
            dma((count,)),
            dma((count,)),
        ],
        compiler_params=pltpu.CompilerParams(
            vmem_limit_bytes=58 * 1024 * 1024, collective_id=1, has_side_effects=True
        ),
        name="core",
    )(
        x,
        gain,
        bounds,
        live,
        stem_kernel,
        mid_depthwise,
        mid_pointwise,
        last_depthwise,
        last_pointwise,
        cotangent,
        proj_weight,
        qkv_weight,
        out_weight,
    )


def per_device(
    size,
    features,
    stem_kernel,
    mid_depthwise,
    mid_pointwise,
    last_depthwise,
    last_pointwise,
    proj_weight,
    norm_gain,
    qkv_weight,
    out_weight,
    cotangent,
    utt_bounds,
    live_blocks,
):
    return core(
        size,
        features.shape[1],
        arranged(features),
        norm_gain.reshape(1, -1),
        utt_bounds.T,
        live_blocks,
        stem_kernel,
        mid_depthwise,
        mid_pointwise,
        last_depthwise,
        last_pointwise,
        cotangent,
        proj_weight,
        qkv_weight,
        out_weight,
    )


def solution(mesh):
    split = P(("groups", "tm"), None)
    in_specs = (split,) + (P(),) * 9 + (split, P("groups", None), split)
    return jax.shard_map(
        functools.partial(per_device, mesh.shape["tm"]),
        mesh=mesh,
        in_specs=in_specs,
        out_specs=(split, split, split),
        check_vma=False,
    )
```

```python
import functools

import jax
import jax.numpy as jnp
from jax import lax
from jax.experimental import pallas as pl
from jax.experimental.pallas import tpu as pltpu
from jax.sharding import PartitionSpec as P

HEADS = 8
REACH = 3
HEAD_DIM = 128
norm_eps = 1e-05
neg_fill = -1e30
MEL_PITCH = 84
SCALE = HEAD_DIM ** (-0.5)
PIECES = 4
PANEL = 128
AHEAD = 2


def dot_nt(a, b):
    return lax.dot_general(a, b, (((1,), (1,)), ((), ())), preferred_element_type=jnp.float32)


def dot_tn(a, b):
    return lax.dot_general(a, b, (((0,), (0,)), ((), ())), preferred_element_type=jnp.float32)


def dot_nn(a, b):
    return jnp.dot(a, b, preferred_element_type=jnp.float32)


MESH = pl.DeviceIdType.MESH


class Exchange:
    def __init__(self, size, out_ref, send, recv):
        self.size, self.out, self.send, self.recv = size, out_ref, send, recv
        self.rows = out_ref.shape[1] // PIECES
        self.me = lax.axis_index("tm")
        self.odd = lax.rem(self.me, 2)
        self.upper = lax.rem(self.me // 2, 2)
        self.sibling = self.me + 1 - 2 * self.odd
        self.beside = self.me + 2 - 4 * self.upper
        self.far = self.me - 3 + 6 * self.odd
        self.onward = self.me + 4 - 8 * self.upper
        self.back = self.me - 4 + 8 * self.upper
        self.has_far = self.inside(self.far)
        self.has_onward = self.inside(self.onward)
        self.has_back = self.inside(self.back)
        self.low = 1 + 4 * self.upper
        self.high = 5 - 4 * self.upper

    def inside(self, target):
        return jnp.logical_and(target >= 0, target < self.size)

    def copy(self, source, slot, sem, target):
        return pltpu.make_async_remote_copy(
            src_ref=self.out.at[source],
            dst_ref=self.out.at[slot],
            send_sem=self.send.at[sem],
            recv_sem=self.recv.at[sem],
            device_id={"tm": target},
            device_id_type=MESH,
        )

    def piece(self, source, slot, sem, target, j):
        span = pl.ds(j * self.rows, self.rows)
        return pltpu.make_async_remote_copy(
            src_ref=self.out.at[source, span, :],
            dst_ref=self.out.at[slot, span, :],
            send_sem=self.send.at[sem],
            recv_sem=self.recv.at[sem],
            device_id={"tm": target},
            device_id_type=MESH,
        )

    def twin(self):
        return self.copy(REACH, 2 + 2 * self.odd, 0, self.sibling)

    def remote(self):
        return self.copy(REACH, 6 - 6 * self.odd, 1, self.far)

    def near(self, j):
        return self.piece(REACH, self.low, 2 + j, self.beside, j)

    def near_in(self, j):
        return self.piece(REACH, self.high, 2 + j, self.beside, j)

    def deep(self, j):
        return self.piece(self.high, self.low, 2 + PIECES + j, self.onward, j)

    def deep_in(self, j):
        return self.piece(REACH, self.low, 2 + PIECES + j, self.back, j)

    def near_pass(self, j):
        slot = 4 - 4 * self.upper + 2 * self.odd
        return self.piece(self.high, slot, 2 + 2 * PIECES + j, self.sibling, j)

    def near_pass_in(self, j):
        slot = 6 - 4 * self.upper - 2 * self.odd
        return self.piece(REACH, slot, 2 + 2 * PIECES + j, self.sibling, j)

    def deep_pass(self, j):
        slot = 4 * self.upper + 2 * self.odd
        return self.piece(self.low, slot, 2 + 3 * PIECES + j, self.sibling, j)

    def deep_pass_in(self, j):
        slot = 4 * self.upper + 2 - 2 * self.odd
        return self.piece(REACH, slot, 2 + 3 * PIECES + j, self.sibling, j)

    def blank(self):
        for slot in range(2 * REACH + 1):
            if slot != REACH:

                @pl.when(jnp.logical_not(self.inside(self.me + slot - REACH)))
                def _(slot=slot):
                    self.out[slot] = jnp.zeros(self.out.shape[1:], self.out.dtype)

    def start(self):
        for j in range(PIECES):
            self.near(j).start()
        pl.when(self.has_far)(lambda: self.remote().start())
        self.twin().start()

    def relay(self, j):
        self.near_in(j).wait_recv()
        pl.when(self.has_onward)(lambda: self.deep(j).start())
        self.near_pass(j).start()

    def relay_deep(self, j):
        @pl.when(self.has_back)
        def _():
            self.deep_in(j).wait_recv()
            self.deep_pass(j).start()

    def near_done(self):
        for j in range(PIECES):
            self.near_pass_in(j).wait_recv()

    def deep_done(self):
        for j in range(PIECES):
            pl.when(self.has_back)(lambda: self.deep_pass_in(j).wait_recv())

    def drain(self):
        self.twin().wait_send()
        pl.when(self.has_far)(lambda: self.remote().wait_send())
        for j in range(PIECES):
            self.near(j).wait_send()
            self.near_pass(j).wait_send()
            pl.when(self.has_onward)(lambda: self.deep(j).wait_send())
            pl.when(self.has_back)(lambda: self.deep_pass(j).wait_send())


def segments(positions, bounds_ref):
    found = jnp.zeros(positions.shape, jnp.int32)
    for u in range(bounds_ref.shape[1]):
        inside = (positions >= bounds_ref[0, u]) & (positions < bounds_ref[1, u])
        found = jnp.where(inside, u + 1, found)
    return found


class Subsample:
    def __init__(self, x, stem_w, mid_dw, mid_w, last_dw, last_w, flat, turned, even, odd, second, shifted, taps):
        self.x, self.stem_w, self.mid_dw, self.mid_w = x, stem_w, mid_dw, mid_w
        self.last_dw, self.last_w, self.flat, self.turned = last_dw, last_w, flat, turned
        self.even, self.odd, self.second, self.shifted, self.taps = even, odd, second, shifted, taps
        self.rows = x.shape[0] // 4
        self.main = self.rows - 8
        self.mids = second.shape[0] - 1
        self.span = shifted.shape[1] - 256

    def blank(self):
        self.odd[0] = jnp.zeros(self.odd.shape[1:], self.odd.dtype)
        self.second[0] = jnp.zeros(self.second.shape[1:], self.second.dtype)
        self.shifted[...] = jnp.zeros(self.shifted.shape, jnp.float32)

    def spread(self):
        for dt in range(3):
            for df in range(3):
                row = 3 * dt + df
                tap = self.stem_w[dt, df : df + 1, :].astype(jnp.float32)
                for i in range(4):
                    at = self.span + 2 * i + dt * MEL_PITCH + df
                    self.shifted[i, at : at + 1, :] = tap
                self.taps[row : row + 1, :] = self.mid_dw[dt, df : df + 1, :].astype(jnp.float32)
                last = self.last_dw[dt, df : df + 1, :].astype(jnp.float32)
                self.taps[16 + row : 17 + row, :] = last

    def step(self, k, half):
        main, rows, second = self.main, self.rows, self.second

        def stem(i):
            start = pl.multiple_of(self.span - 8 * k, 8)
            taps = self.shifted[i, pl.ds(start, 256), :].astype(jnp.bfloat16)
            return jnp.maximum(dot_nn(self.x[...], taps), 0.0).reshape(self.even.shape)

        m = 2 * k + half
        self.even[...] = stem(2 * half)
        self.odd[1 - half] = stem(2 * half + 1)
        parts = (self.odd.at[half], self.even, self.odd.at[1 - half])
        early = jnp.zeros((main, 256), jnp.float32)
        late = jnp.zeros((rows, 256), jnp.float32)
        for df in range(3):
            part = parts[df]
            for dt in range(3):
                tap = self.taps[3 * dt + df : 3 * dt + df + 1, :]
                phase = (3, 0, 1)[dt]
                start = 7 if dt == 0 else 8
                early += part[phase, start : start + main, :] * tap
                late += part[dt + 1] * tap
        weight = self.mid_w[...]
        second[m + 1, 0, 8:rows, :] = jnp.maximum(dot_nn(early.astype(jnp.bfloat16), weight), 0.0)
        second[m + 1, 1] = jnp.maximum(dot_nn(late.astype(jnp.bfloat16), weight), 0.0)

    def run(self, first, last):
        def body(k, _):
            self.step(k, 0)
            self.step(k, 1)
            return 0

        lax.fori_loop(first, last, body, 0)

    def finish(self, f):
        total = jnp.zeros((self.main, 256), jnp.float32)
        for df in range(3):
            for dt in range(3):
                tap = self.taps[16 + 3 * dt + df : 17 + 3 * dt + df, :]
                phase = (1, 0, 1)[dt]
                start = 7 if dt == 0 else 8
                total += self.second[2 * f + df, phase, start : start + self.main, :] * tap
        out = jnp.maximum(dot_nn(total.astype(jnp.bfloat16), self.last_w[...]), 0.0)
        self.flat[:, f * 256 : (f + 1) * 256] = out.astype(jnp.bfloat16)
        self.turned[f * 256 : (f + 1) * 256, :] = out.T.astype(jnp.bfloat16)


class Half:
    def __init__(self, size):
        self.size, self.half = size, size // 2
        self.me = lax.axis_index("tm")
        self.base = self.me // self.half * self.half
        self.own = self.me - self.base
        self.partner = self.half - self.base + self.own
        self.core = lax.rem(self.me, 2)
        self.sibling = self.me + 1 - 2 * self.core
        self.across = self.me + 2 - 4 * lax.rem(self.me // 2, 2)
        self.steps = self.half // 4

    def turn(self, slot, step):
        return lax.rem(slot + 4 * step, self.half)

    def peer(self, distance):
        return self.base + lax.rem(self.own + distance, self.half)


def core_kernel(
    size,
    gain_ref,
    bounds_ref,
    live_ref,
    features_hbm,
    stem_hbm,
    mid_dw_hbm,
    mid_w_hbm,
    last_dw_hbm,
    last_w_hbm,
    cot_hbm,
    proj_hbm,
    qkv_hbm,
    out_hbm,
    block_out_hbm,
    frame_grads_hbm,
    proj_grads_hbm,
    block_out_ref,
    frame_grads_ref,
    proj_grads_ref,
    stem_w,
    mid_dw,
    mid_w,
    last_dw,
    last_w,
    turned_features,
    feature_rows,
    x_own,
    halo_out,
    halo_in,
    flat_ref,
    turned_ref,
    even,
    odd_part,
    second,
    shifted,
    taps,
    cot_ref,
    proj_w,
    qkv_w,
    out_w,
    xw,
    do_ref,
    pj,
    mixed_ref,
    grads_ref,
    bias_ref,
    stat_ref,
    normalized_ref,
    panels,
    columns,
    out_part,
    in_part,
    load_sem,
    halo_sem,
    cot_send,
    cot_recv,
    send,
    recv,
    stat_send,
    stat_recv,
    col_send,
    col_recv,
    panel_send,
    panel_recv,
    part_send,
    part_recv,
    out_sem,
):
    rows, width = block_out_ref.shape
    window = (2 * REACH + 1) * rows
    depth = flat_ref.shape[1]
    share = depth // size
    count = width // PANEL
    me = lax.axis_index("tm")
    half = Half(size)
    cot_exchange = Exchange(size, cot_ref, cot_send, cot_recv)
    exchange = Exchange(size, xw, send, recv)
    odd = exchange.odd
    offsets = [o for o in range(-REACH, REACH + 1) if o]
    conv = Subsample(
        x_own, stem_w, mid_dw, mid_w, last_dw, last_w, flat_ref, turned_ref, even, odd_part, second, shifted, taps
    )

    def load(i, source, target):
        return pltpu.make_async_copy(source, target, load_sem.at[i])

    small = [
        load(0, cot_hbm, cot_ref.at[REACH]),
        load(1, stem_hbm, stem_w),
        load(2, mid_dw_hbm, mid_dw),
        load(3, mid_w_hbm, mid_w),
        load(4, last_dw_hbm, last_dw),
        load(5, last_w_hbm, last_w),
    ]
    series = load(9, features_hbm, turned_features)
    series.start()
    large = [load(6, proj_hbm, proj_w), load(7, out_hbm, out_w), load(8, qkv_hbm, qkv_w)]
    for item in small:
        item.start()

    barrier = pltpu.get_barrier_semaphore()
    peers = 0
    for distance in range(1, size):
        other = lax.rem(me + distance, size)
        gap = other - me
        near = jnp.logical_and(gap >= -4, gap <= 4)
        same = other // half.half == me // half.half
        known = jnp.logical_or(jnp.logical_or(near, same), other == half.partner)
        peers += jnp.where(known, 1, 0)

        @pl.when(known)
        def _(other=other):
            pl.semaphore_signal(barrier, inc=1, device_id={"tm": other}, device_id_type=MESH)

    def there(offset):
        return jnp.logical_and(me + offset >= 0, me + offset < size)

    def when_there(offset, action):
        pl.when(there(offset))(lambda: action(offset))

    for offset in offsets:

        @pl.when(jnp.logical_not(there(offset)))
        def _(offset=offset):
            stat_ref[REACH + offset] = jnp.zeros(stat_ref.shape[1:], jnp.float32)

    slab = conv.rows
    conv.blank()
    series.wait()
    mel, times = turned_features.shape
    tall = jnp.concatenate(
        [turned_features[...].astype(jnp.float32), jnp.zeros((128 - mel, times), jnp.float32)], axis=0
    )
    feature_rows[...] = tall.T
    phases = [feature_rows[pl.ds(i, rows, stride=8), :] for i in range(8)]
    first_row = lax.broadcasted_iota(jnp.int32, (rows, 128), 0) == 0
    before = jnp.where(first_row, 0.0, pltpu.roll(phases[7], 1, 0))
    empty = jnp.zeros((rows, 128), jnp.float32)

    def lanes_at(part, dt):
        return pltpu.roll(jnp.concatenate([part, empty], axis=1), dt * MEL_PITCH + 1, 1)

    slabs = []
    for p in range(4):
        parts = [before if p == 0 else phases[2 * p - 1], phases[2 * p], phases[2 * p + 1]]
        built = sum(lanes_at(part, dt) for dt, part in enumerate(parts))
        tail = built[rows - 8 : rows]
        halo_out[8 * p : 8 * p + 8, :] = tail
        if p == 3:
            halo_out[32:40, :] = pltpu.roll(tail, 256 - 2 * MEL_PITCH, 1)
        slabs += [jnp.zeros((8, 256), jnp.float32), built]
    x_own[...] = jnp.concatenate(slabs, axis=0).astype(jnp.bfloat16)

    @pl.when(me == 0)
    def _():
        halo_in[...] = jnp.zeros(halo_in.shape, jnp.float32)

    def halo(target):
        return pltpu.make_async_remote_copy(
            src_ref=halo_out,
            dst_ref=halo_in,
            send_sem=halo_sem.at[0],
            recv_sem=halo_sem.at[1],
            device_id={"tm": target},
            device_id_type=MESH,
        )

    small[0].wait()
    pl.semaphore_wait(barrier, peers)
    pl.when(me + 1 < size)(lambda: halo(me + 1).start())
    cot_exchange.start()
    for item in large:
        item.start()
    for item in small[1:]:
        item.wait()
    conv.spread()
    cot_exchange.blank()
    exchange.blank()
    pl.when(me > 0)(lambda: halo(me - 1).wait_recv())
    place = lax.broadcasted_iota(jnp.int32, (8, 256), 0)
    lane = lax.broadcasted_iota(jnp.int32, (8, 256), 1)
    for p in range(4):
        top = x_own[p * slab : p * slab + 16, :].astype(jnp.float32)
        upper = jnp.where(place == 7, halo_in[8 * p : 8 * p + 8, :], top[0:8])
        lower = top[8:16]
        if p == 0:
            carried = jnp.broadcast_to(halo_in[39:40, :], (8, 256))
            lower = jnp.where((place == 0) & (lane < MEL_PITCH), carried, lower)
        x_own[p * slab : p * slab + 16, :] = jnp.concatenate([upper, lower], axis=0).astype(jnp.bfloat16)

    turns = conv.mids // 2
    marks = [turns * (i + 2) // (PIECES + 2) for i in range(PIECES + 1)]
    done = 0
    for j in range(PIECES):
        conv.run(done, marks[j])
        done = marks[j]
        cot_exchange.relay(j)
    conv.run(done, turns)
    for f in range(turns):
        conv.finish(f)
        if f >= 2 and f - 2 < PIECES:
            cot_exchange.relay_deep(f - 2)

    large[0].wait()
    frames = dot_nn(flat_ref[...], proj_w[...]).astype(jnp.bfloat16)
    frames_f = frames.astype(jnp.float32)
    centered = frames_f - jnp.mean(frames_f, axis=-1, keepdims=True)
    inv_std = lax.rsqrt(jnp.mean(centered * centered, axis=-1, keepdims=True) + norm_eps)
    normalized = centered * inv_std
    normalized_ref[...] = normalized
    block_out_ref[...] = frames
    xw[REACH] = (normalized * gain_ref[...]).astype(jnp.bfloat16)
    exchange.start()
    large[1].wait()
    cot_exchange.near_done()
    cot_exchange.deep_done()
    cot_exchange.twin().wait_recv()
    pl.when(cot_exchange.has_far)(lambda: cot_exchange.remote().wait_recv())
    cots = cot_ref[...].reshape(window, width)

    def d_attention(first, last):
        for i in range(first, last, 256):
            do_ref[:, i : i + 256] = dot_nt(cots, out_w[i : i + 256, :]).astype(jnp.bfloat16)

    first = (me - REACH) * rows
    own_col = segments(me * rows + lax.broadcasted_iota(jnp.int32, (rows, 128), 0), bounds_ref)
    for b in range(2 * REACH + 1):
        place = first + b * rows
        live = live_ref[0, b] == 1
        row = segments(place + lax.broadcasted_iota(jnp.int32, (8, rows), 1), bounds_ref)[0:1]
        same = (own_col[:, 0:1] == row) & live
        bias_ref[:, b * rows : (b + 1) * rows] = jnp.where(same, 0.0, neg_fill)

    def turned(target):
        start = pl.multiple_of(target * share, 16)
        return turned_ref.at[pl.ds(start, share), :]

    def landing(which, slot):
        start = pl.multiple_of(slot * rows, rows)
        return columns.at[pl.ds(which * share, share), pl.ds(start, rows)]

    def column(which, distance):
        target = half.peer(distance)
        other = target if which == 0 else lax.rem(target + half.half, size)
        return pltpu.make_async_remote_copy(
            src_ref=turned(other),
            dst_ref=landing(which, half.own),
            send_sem=col_send.at[which, distance],
            recv_sem=col_recv.at[which, distance],
            device_id={"tm": target},
            device_id_type=MESH,
        )

    def column_in(which, distance):
        slot = lax.rem(half.own - distance + half.half, half.half)
        return pltpu.make_async_remote_copy(
            src_ref=turned(me),
            dst_ref=landing(which, slot),
            send_sem=col_send.at[which, distance],
            recv_sem=col_recv.at[which, distance],
            device_id={"tm": half.peer(distance)},
            device_id_type=MESH,
        )

    def column_own(which):
        other = me if which == 0 else half.partner
        return pltpu.make_async_copy(turned(other), landing(which, half.own), col_send.at[which, 0])

    large[2].wait()

    def project(slot, blocks, first, last):
        x = xw[pl.ds(slot, blocks)].reshape(blocks * rows, width)
        for i in range(first, last, 512):
            out = dot_nn(x, qkv_w[:, i : i + 512]).astype(jnp.bfloat16)
            start = pl.multiple_of(slot * rows, rows)
            pj[pl.ds(start, blocks * rows), i : i + 512] = out

    d_attention(0, width // 2)
    exchange.relay(0)
    exchange.twin().wait_recv()
    project(REACH - odd, 2, 0, 3 * width // 2)
    exchange.relay(1)
    project(REACH - odd, 2, 3 * width // 2, 3 * width)
    exchange.relay(2)
    exchange.relay_deep(0)
    d_attention(width // 2, width)
    exchange.relay(3)
    exchange.relay_deep(1)
    for which in range(0, 1):
        column_own(which).start()
        for distance in range(1, half.half):
            column(which, distance).start()
    near_slot = (1 - odd) * exchange.upper + (5 - odd) * (1 - exchange.upper)
    deep_slot = (5 - odd) * exchange.upper + (1 - odd) * (1 - exchange.upper)
    pl.when(exchange.has_far)(lambda: exchange.remote().wait_recv())
    project(6 * odd, 1, 0, 3 * width)
    exchange.near_done()
    exchange.relay_deep(2)
    project(near_slot, 2, 0, 3 * width // 2)
    exchange.relay_deep(3)
    project(near_slot, 2, 3 * width // 2, 3 * width)
    exchange.deep_done()
    project(deep_slot, 2, 0, 3 * width)

    own = slice(REACH * rows, (REACH + 1) * rows)
    lanes = lax.broadcasted_iota(jnp.int32, (rows, 128), 1)

    def head(group, h):
        return pl.ds(pl.multiple_of(group * width + h * HEAD_DIM, HEAD_DIM), HEAD_DIM)

    def forward(h, stats):
        keys = pj[:, head(1, h)]
        values = pj[:, head(2, h)]
        scores = dot_nt(pj[own, head(0, h)], keys) * SCALE + bias_ref[...]
        dprob = dot_nt(do_ref[own, head(0, h)], values)
        top = jnp.max(scores, axis=1, keepdims=True)
        weights = jnp.exp(scores - top)
        mass = jnp.sum(weights, axis=1, keepdims=True)
        probs = weights * (1.0 / mass)
        delta = jnp.sum(probs * dprob, axis=1, keepdims=True)
        dscore = (probs * (dprob - delta)).astype(jnp.bfloat16)
        mixed_ref[:, head(0, h)] = dot_nn(probs.astype(jnp.bfloat16), values).astype(jnp.bfloat16)
        grads_ref[:, head(0, h)] = (dot_nn(dscore, keys) * SCALE).astype(jnp.bfloat16)
        stats = jnp.where(lanes == h, top + jnp.log(mass), stats)
        return jnp.where(lanes == HEADS + h, delta, stats)

    stats = lax.fori_loop(0, HEADS, forward, jnp.zeros((rows, 128), jnp.float32))
    stat_ref[REACH] = stats.T[0 : 2 * HEADS, :]

    def stat_copy(offset, slot, sem):
        return pltpu.make_async_remote_copy(
            src_ref=stat_ref.at[REACH],
            dst_ref=stat_ref.at[slot],
            send_sem=stat_send.at[REACH + offset],
            recv_sem=stat_recv.at[sem],
            device_id={"tm": me + offset},
            device_id_type=MESH,
        )

    def stat_out(offset):
        return stat_copy(offset, REACH - offset, REACH - offset)

    def stat_in(offset):
        return stat_copy(offset, REACH + offset, REACH + offset)

    for offset in offsets:
        when_there(offset, lambda o: stat_out(o).start())
    block_out_ref[...] = (
        block_out_ref[...].astype(jnp.float32) + dot_nn(mixed_ref[...], out_w[...])
    ).astype(jnp.bfloat16)
    stores = [
        pltpu.make_async_copy(block_out_ref, block_out_hbm, out_sem.at[0]),
        pltpu.make_async_copy(frame_grads_ref, frame_grads_hbm, out_sem.at[1]),
        pltpu.make_async_copy(proj_grads_ref, proj_grads_hbm, out_sem.at[2]),
    ]
    stores[0].start()
    grad_normed = dot_nt(grads_ref[:, 0:width], qkv_w[:, 0:width])
    for offset in offsets:
        when_there(offset, lambda o: stat_in(o).wait_recv())

    for which in range(1, 2):
        column_own(which).start()
        for distance in range(1, half.half):
            column(which, distance).start()

    def key_pass(h, _):
        queries = pj[:, head(0, h)]
        douts = do_ref[:, head(0, h)]
        blocks = range(2 * REACH + 1)
        log_norms = jnp.concatenate([stat_ref[b, pl.ds(h, 1), :] for b in blocks], axis=1)
        deltas = jnp.concatenate([stat_ref[b, pl.ds(HEADS + h, 1), :] for b in blocks], axis=1)
        scores = dot_nt(pj[own, head(1, h)], queries) * SCALE + bias_ref[...]
        dprob = dot_nt(pj[own, head(2, h)], douts)
        weights = jnp.exp(scores - log_norms)
        dscore = (weights * (dprob - deltas)).astype(jnp.bfloat16)
        grads_ref[:, head(1, h)] = (dot_nn(dscore, queries) * SCALE).astype(jnp.bfloat16)
        grads_ref[:, head(2, h)] = dot_nn(weights.astype(jnp.bfloat16), douts).astype(jnp.bfloat16)
        return 0

    lax.fori_loop(0, HEADS, key_pass, 0)
    grad_normed += dot_nt(grads_ref[:, width:], qkv_w[:, width:])
    normalized = normalized_ref[...]
    scaled = grad_normed * gain_ref[...]
    ln_grad = inv_std * (
        scaled
        - jnp.mean(scaled, axis=-1, keepdims=True)
        - normalized * jnp.mean(scaled * normalized, axis=-1, keepdims=True)
    )
    frame_grads = (cot_ref[REACH].astype(jnp.float32) + ln_grad).astype(jnp.bfloat16)
    for p in range(count):
        panels[p, half.own] = frame_grads[:, p * PANEL : (p + 1) * PANEL]

    def panel(p, slot, sem, target):
        return pltpu.make_async_remote_copy(
            src_ref=panels.at[p, slot],
            dst_ref=panels.at[p, slot],
            send_sem=panel_send.at[p, sem],
            recv_sem=panel_recv.at[p, sem],
            device_id={"tm": target},
            device_id_type=MESH,
        )

    steps = half.steps
    flip = half.across - half.me
    twin = half.sibling - half.me

    def along(p, s):
        return panel(p, half.own, s, half.base + half.turn(half.own, s))

    def along_in(p, s):
        return panel(p, half.turn(half.own, steps - s), s, half.base + half.turn(half.own, s))

    def cross(p, s):
        return panel(p, half.turn(half.own, steps - s), steps + s, half.across)

    def cross_in(p, s):
        return panel(p, half.turn(half.own, steps - s) + flip, steps + s, half.across)

    def twin_near(p, s):
        return panel(p, half.turn(half.own, steps - s), 2 * steps + s, half.sibling)

    def twin_near_in(p, s):
        return panel(p, half.turn(half.own, steps - s) + twin, 2 * steps + s, half.sibling)

    def twin_far(p, s):
        return panel(p, half.turn(half.own, steps - s) + flip, 3 * steps + s, half.sibling)

    def twin_far_in(p, s):
        return panel(p, half.turn(half.own, steps - s) + flip + twin, 3 * steps + s, half.sibling)

    def part(p):
        return pltpu.make_async_remote_copy(
            src_ref=out_part.at[p],
            dst_ref=in_part.at[p],
            send_sem=part_send.at[p],
            recv_sem=part_recv.at[p],
            device_id={"tm": half.partner},
            device_id_type=MESH,
        )

    def relay(p):
        for s in range(1, steps):
            along_in(p, s).wait_recv()
            cross(p, s).start()
            twin_near(p, s).start()

    def share_far(p):
        for s in range(steps):
            cross_in(p, s).wait_recv()
            twin_far(p, s).start()

    def multiply(p):
        for s in range(steps):
            twin_near_in(p, s).wait_recv()
            twin_far_in(p, s).wait_recv()
        sums = dot_nn(columns[...], panels[p].reshape(half.half * rows, PANEL))
        out_part[p] = sums[share:].astype(jnp.bfloat16)
        part(p).start()
        proj_grads_ref[:, p * PANEL : (p + 1) * PANEL] = sums[:share]

    for p in range(count):
        for s in range(1, steps):
            along(p, s).start()
        if p < AHEAD:
            cross(p, 0).start()
        twin_near(p, 0).start()
    frame_grads_ref[...] = frame_grads
    stores[1].start()
    for which in range(2):
        column_own(which).wait()
        for distance in range(1, half.half):
            column_in(which, distance).wait_recv()
    for t in range(count + 2):
        if t < count:
            relay(t)
            if t + AHEAD < count:
                cross(t + AHEAD, 0).start()
        if 1 <= t <= count:
            share_far(t - 1)
        if t >= 2:
            multiply(t - 2)
    for p in range(count):
        part(p).wait_recv()
        span = slice(p * PANEL, (p + 1) * PANEL)
        proj_grads_ref[:, span] = proj_grads_ref[:, span] + in_part[p].astype(jnp.float32)

    stores[2].start()
    cot_exchange.drain()
    exchange.drain()
    pl.when(me + 1 < size)(lambda: halo(me + 1).wait_send())
    for offset in offsets:
        when_there(offset, lambda o: stat_out(o).wait_send())
    for which in range(2):
        for distance in range(1, half.half):
            column(which, distance).wait_send()
    for p in range(count):
        for s in range(1, steps):
            along(p, s).wait_send()
        for s in range(steps):
            cross(p, s).wait_send()
            twin_near(p, s).wait_send()
            twin_far(p, s).wait_send()
        part(p).wait_send()
    for store in stores:
        store.wait()


def finish_kernel(a_ref, b_ref, c_ref, a_out, b_out, c_out, a_held, b_held, c_held, sem):
    held = (a_held, b_held, c_held)
    reads = [pltpu.make_async_copy(r, h, sem.at[i]) for i, (r, h) in enumerate(zip((a_ref, b_ref, c_ref), held))]
    writes = [pltpu.make_async_copy(h, o, sem.at[3 + i]) for i, (h, o) in enumerate(zip(held, (a_out, b_out, c_out)))]
    for item in reads:
        item.start()
    for read, write in zip(reads, writes):
        read.wait()
        write.start()
    for item in writes:
        item.wait()


def finished(arrays):
    hbm = pl.BlockSpec(memory_space=pl.ANY)
    return pl.pallas_call(
        finish_kernel,
        out_shape=tuple(jax.ShapeDtypeStruct(a.shape, a.dtype) for a in arrays),
        in_specs=[hbm] * 3,
        out_specs=(hbm,) * 3,
        scratch_shapes=[pltpu.VMEM(a.shape, a.dtype) for a in arrays] + [pltpu.SemaphoreType.DMA((6,))],
        name="finish",
    )(*arrays)


def core(
    size,
    features,
    gain,
    bounds,
    live,
    stem_kernel,
    mid_depthwise,
    mid_pointwise,
    last_depthwise,
    last_pointwise,
    cotangent,
    proj_weight,
    qkv_weight,
    out_weight,
):
    rows = cotangent.shape[0]
    slab = rows + 8
    mel = features.shape[0]
    mids = mel // 4
    channels = stem_kernel.shape[-1]
    depth, width = proj_weight.shape
    share = depth // size
    half = size // 2
    steps = half // 4
    count = width // PANEL
    blocks = 2 * REACH + 1
    vmem = pl.BlockSpec(memory_space=pltpu.VMEM)
    smem = pl.BlockSpec(memory_space=pltpu.SMEM)
    hbm = pl.BlockSpec(memory_space=pl.ANY)
    dma = pltpu.SemaphoreType.DMA
    bf16, f32 = jnp.bfloat16, jnp.float32
    return pl.pallas_call(
        functools.partial(core_kernel, size),
        out_shape=(
            jax.ShapeDtypeStruct((rows, width), bf16),
            jax.ShapeDtypeStruct((rows, width), bf16),
            jax.ShapeDtypeStruct((share, width), f32),
        ),
        in_specs=[vmem] + [smem] * 2 + [hbm] * 10,
        out_specs=(hbm,) * 3,
        scratch_shapes=[
            pltpu.VMEM((rows, width), bf16),
            pltpu.VMEM((rows, width), bf16),
            pltpu.VMEM((share, width), f32),
            pltpu.VMEM(stem_kernel.shape, bf16),
            pltpu.VMEM(mid_depthwise.shape, bf16),
            pltpu.VMEM(mid_pointwise.shape, bf16),
            pltpu.VMEM(last_depthwise.shape, bf16),
            pltpu.VMEM(last_pointwise.shape, bf16),
            pltpu.VMEM(features.shape, bf16),
            pltpu.VMEM((features.shape[1], 128), f32),
            pltpu.VMEM((4 * slab, 256), bf16),
            pltpu.VMEM((40, 256), f32),
            pltpu.VMEM((40, 256), f32),
            pltpu.VMEM((rows, depth), bf16),
            pltpu.VMEM((depth, rows), bf16),
            pltpu.VMEM((4, slab, channels), f32),
            pltpu.VMEM((2, 4, slab, channels), f32),
            pltpu.VMEM((mids + 1, 2, slab, channels), f32),
            pltpu.VMEM((4, mel + 256, channels), f32),
            pltpu.VMEM((32, channels), f32),
            pltpu.VMEM((blocks, rows, width), bf16),
            pltpu.VMEM(proj_weight.shape, bf16),
            pltpu.VMEM(qkv_weight.shape, bf16),
            pltpu.VMEM(out_weight.shape, bf16),
            pltpu.VMEM((blocks, rows, width), bf16),
            pltpu.VMEM((blocks * rows, width), bf16),
            pltpu.VMEM((blocks * rows, 3 * width), bf16),
            pltpu.VMEM((rows, width), bf16),
            pltpu.VMEM((rows, 3 * width), bf16),
            pltpu.VMEM((rows, blocks * rows), f32),
            pltpu.VMEM((blocks, 2 * HEADS, rows), f32),
            pltpu.VMEM((rows, width), f32),
            pltpu.VMEM((count, half, rows, PANEL), bf16),
            pltpu.VMEM((2 * share, half * rows), bf16),
            pltpu.VMEM((count, share, PANEL), bf16),
            pltpu.VMEM((count, share, PANEL), bf16),
            dma((10,)),
            dma((2,)),
            dma((2 + 4 * PIECES,)),
            dma((2 + 4 * PIECES,)),
            dma((2 + 4 * PIECES,)),
            dma((2 + 4 * PIECES,)),
            dma((blocks,)),
            dma((blocks,)),
            dma((2, half)),
            dma((2, half)),
            dma((count, 4 * steps)),
            dma((count, 4 * steps)),
            dma((count,)),
            dma((count,)),
            dma((3,)),
        ],
        compiler_params=pltpu.CompilerParams(
            vmem_limit_bytes=58 * 1024 * 1024, collective_id=1, has_side_effects=True
        ),
        name="core",
    )(
        gain,
        bounds,
        live,
        features,
        stem_kernel,
        mid_depthwise,
        mid_pointwise,
        last_depthwise,
        last_pointwise,
        cotangent,
        proj_weight,
        qkv_weight,
        out_weight,
    )


def per_device(
    size,
    features,
    stem_kernel,
    mid_depthwise,
    mid_pointwise,
    last_depthwise,
    last_pointwise,
    proj_weight,
    norm_gain,
    qkv_weight,
    out_weight,
    cotangent,
    utt_bounds,
    live_blocks,
):
    results = core(
        size,
        features.T,
        norm_gain.reshape(1, -1),
        utt_bounds.T,
        live_blocks,
        stem_kernel,
        mid_depthwise,
        mid_pointwise,
        last_depthwise,
        last_pointwise,
        cotangent,
        proj_weight,
        qkv_weight,
        out_weight,
    )
    return finished(results)


def solution(mesh):
    split = P(("groups", "tm"), None)
    in_specs = (split,) + (P(),) * 9 + (split, P("groups", None), split)
    return jax.shard_map(
        functools.partial(per_device, mesh.shape["tm"]),
        mesh=mesh,
        in_specs=in_specs,
        out_specs=(split, split, split),
        check_vma=False,
    )
```

```python
import functools

import jax
import jax.numpy as jnp
from jax import lax
from jax.experimental import pallas as pl
from jax.experimental.pallas import tpu as pltpu
from jax.sharding import PartitionSpec as P

HEADS = 8
REACH = 3
HEAD_DIM = 128
norm_eps = 1e-05
neg_fill = -1e30
MEL_PITCH = 84
SCALE = HEAD_DIM ** (-0.5)
PIECES = 4
PANEL = 128
AHEAD = 4
DIRECT = 4


def dot_nt(a, b):
    return lax.dot_general(a, b, (((1,), (1,)), ((), ())), preferred_element_type=jnp.float32)


def dot_tn(a, b):
    return lax.dot_general(a, b, (((0,), (0,)), ((), ())), preferred_element_type=jnp.float32)


def dot_nn(a, b):
    return jnp.dot(a, b, preferred_element_type=jnp.float32)


MESH = pl.DeviceIdType.MESH


class Exchange:
    def __init__(self, size, out_ref, send, recv):
        self.size, self.out, self.send, self.recv = size, out_ref, send, recv
        self.rows = out_ref.shape[1] // PIECES
        self.me = lax.axis_index("tm")
        self.odd = lax.rem(self.me, 2)
        self.upper = lax.rem(self.me // 2, 2)
        self.sibling = self.me + 1 - 2 * self.odd
        self.beside = self.me + 2 - 4 * self.upper
        self.far = self.me - 3 + 6 * self.odd
        self.onward = self.me + 4 - 8 * self.upper
        self.back = self.me - 4 + 8 * self.upper
        self.has_far = self.inside(self.far)
        self.has_onward = self.inside(self.onward)
        self.has_back = self.inside(self.back)
        self.low = 1 + 4 * self.upper
        self.high = 5 - 4 * self.upper

    def inside(self, target):
        return jnp.logical_and(target >= 0, target < self.size)

    def copy(self, source, slot, sem, target):
        return pltpu.make_async_remote_copy(
            src_ref=self.out.at[source],
            dst_ref=self.out.at[slot],
            send_sem=self.send.at[sem],
            recv_sem=self.recv.at[sem],
            device_id={"tm": target},
            device_id_type=MESH,
        )

    def piece(self, source, slot, sem, target, j):
        span = pl.ds(j * self.rows, self.rows)
        return pltpu.make_async_remote_copy(
            src_ref=self.out.at[source, span, :],
            dst_ref=self.out.at[slot, span, :],
            send_sem=self.send.at[sem],
            recv_sem=self.recv.at[sem],
            device_id={"tm": target},
            device_id_type=MESH,
        )

    def twin(self):
        return self.copy(REACH, 2 + 2 * self.odd, 0, self.sibling)

    def remote(self):
        return self.copy(REACH, 6 - 6 * self.odd, 1, self.far)

    def near(self, j):
        return self.piece(REACH, self.low, 2 + j, self.beside, j)

    def near_in(self, j):
        return self.piece(REACH, self.high, 2 + j, self.beside, j)

    def deep(self, j):
        return self.piece(self.high, self.low, 2 + PIECES + j, self.onward, j)

    def deep_in(self, j):
        return self.piece(REACH, self.low, 2 + PIECES + j, self.back, j)

    def near_pass(self, j):
        slot = 4 - 4 * self.upper + 2 * self.odd
        return self.piece(self.high, slot, 2 + 2 * PIECES + j, self.sibling, j)

    def near_pass_in(self, j):
        slot = 6 - 4 * self.upper - 2 * self.odd
        return self.piece(REACH, slot, 2 + 2 * PIECES + j, self.sibling, j)

    def deep_pass(self, j):
        slot = 4 * self.upper + 2 * self.odd
        return self.piece(self.low, slot, 2 + 3 * PIECES + j, self.sibling, j)

    def deep_pass_in(self, j):
        slot = 4 * self.upper + 2 - 2 * self.odd
        return self.piece(REACH, slot, 2 + 3 * PIECES + j, self.sibling, j)

    def blank(self):
        for slot in range(2 * REACH + 1):
            if slot != REACH:

                @pl.when(jnp.logical_not(self.inside(self.me + slot - REACH)))
                def _(slot=slot):
                    self.out[slot] = jnp.zeros(self.out.shape[1:], self.out.dtype)

    def start(self):
        for j in range(PIECES):
            self.near(j).start()
        pl.when(self.has_far)(lambda: self.remote().start())
        self.twin().start()

    def relay(self, j):
        self.near_in(j).wait_recv()
        pl.when(self.has_onward)(lambda: self.deep(j).start())
        self.near_pass(j).start()

    def relay_deep(self, j):
        @pl.when(self.has_back)
        def _():
            self.deep_in(j).wait_recv()
            self.deep_pass(j).start()

    def near_done(self):
        for j in range(PIECES):
            self.near_pass_in(j).wait_recv()

    def deep_done(self):
        for j in range(PIECES):
            pl.when(self.has_back)(lambda: self.deep_pass_in(j).wait_recv())

    def drain(self):
        self.twin().wait_send()
        pl.when(self.has_far)(lambda: self.remote().wait_send())
        for j in range(PIECES):
            self.near(j).wait_send()
            self.near_pass(j).wait_send()
            pl.when(self.has_onward)(lambda: self.deep(j).wait_send())
            pl.when(self.has_back)(lambda: self.deep_pass(j).wait_send())


def segments(positions, bounds_ref):
    found = jnp.zeros(positions.shape, jnp.int32)
    for u in range(bounds_ref.shape[1]):
        inside = (positions >= bounds_ref[0, u]) & (positions < bounds_ref[1, u])
        found = jnp.where(inside, u + 1, found)
    return found


class Subsample:
    def __init__(self, x, stem_w, mid_dw, mid_w, last_dw, last_w, flat, turned, even, odd, second, shifted, taps):
        self.x, self.stem_w, self.mid_dw, self.mid_w = x, stem_w, mid_dw, mid_w
        self.last_dw, self.last_w, self.flat, self.turned = last_dw, last_w, flat, turned
        self.even, self.odd, self.second, self.shifted, self.taps = even, odd, second, shifted, taps
        self.rows = x.shape[0] // 4
        self.main = self.rows - 8
        self.mids = second.shape[0] - 1
        self.span = shifted.shape[1] - 256

    def blank(self):
        self.odd[0] = jnp.zeros(self.odd.shape[1:], self.odd.dtype)
        self.second[0] = jnp.zeros(self.second.shape[1:], self.second.dtype)
        self.shifted[...] = jnp.zeros(self.shifted.shape, jnp.float32)

    def spread(self):
        for dt in range(3):
            for df in range(3):
                row = 3 * dt + df
                tap = self.stem_w[dt, df : df + 1, :].astype(jnp.float32)
                for i in range(4):
                    at = self.span + 2 * i + dt * MEL_PITCH + df
                    self.shifted[i, at : at + 1, :] = tap
                self.taps[row : row + 1, :] = self.mid_dw[dt, df : df + 1, :].astype(jnp.float32)
                last = self.last_dw[dt, df : df + 1, :].astype(jnp.float32)
                self.taps[16 + row : 17 + row, :] = last

    def step(self, k, half):
        main, rows, second = self.main, self.rows, self.second

        def stem(i):
            start = pl.multiple_of(self.span - 8 * k, 8)
            taps = self.shifted[i, pl.ds(start, 256), :].astype(jnp.bfloat16)
            return jnp.maximum(dot_nn(self.x[...], taps), 0.0).reshape(self.even.shape)

        m = 2 * k + half
        self.even[...] = stem(2 * half)
        self.odd[1 - half] = stem(2 * half + 1)
        parts = (self.odd.at[half], self.even, self.odd.at[1 - half])
        early = jnp.zeros((main, 256), jnp.float32)
        late = jnp.zeros((rows, 256), jnp.float32)
        for df in range(3):
            part = parts[df]
            for dt in range(3):
                tap = self.taps[3 * dt + df : 3 * dt + df + 1, :]
                phase = (3, 0, 1)[dt]
                start = 7 if dt == 0 else 8
                early += part[phase, start : start + main, :] * tap
                late += part[dt + 1] * tap
        weight = self.mid_w[...]
        second[m + 1, 0, 8:rows, :] = jnp.maximum(dot_nn(early.astype(jnp.bfloat16), weight), 0.0)
        second[m + 1, 1] = jnp.maximum(dot_nn(late.astype(jnp.bfloat16), weight), 0.0)

    def run(self, first, last):
        def body(k, _):
            self.step(k, 0)
            self.step(k, 1)
            return 0

        lax.fori_loop(first, last, body, 0, unroll=True)

    def finish(self, f):
        total = jnp.zeros((self.main, 256), jnp.float32)
        for df in range(3):
            for dt in range(3):
                tap = self.taps[16 + 3 * dt + df : 17 + 3 * dt + df, :]
                phase = (1, 0, 1)[dt]
                start = 7 if dt == 0 else 8
                total += self.second[2 * f + df, phase, start : start + self.main, :] * tap
        out = jnp.maximum(dot_nn(total.astype(jnp.bfloat16), self.last_w[...]), 0.0)
        self.flat[:, f * 256 : (f + 1) * 256] = out.astype(jnp.bfloat16)
        self.turned[f * 256 : (f + 1) * 256, :] = out.T.astype(jnp.bfloat16)


class Half:
    def __init__(self, size):
        self.size, self.half = size, size // 2
        self.me = lax.axis_index("tm")
        self.base = self.me // self.half * self.half
        self.own = self.me - self.base
        self.partner = self.half - self.base + self.own
        self.core = lax.rem(self.me, 2)
        self.sibling = self.me + 1 - 2 * self.core
        self.across = self.me + 2 - 4 * lax.rem(self.me // 2, 2)
        self.steps = self.half // 4

    def turn(self, slot, step):
        return lax.rem(slot + 4 * step, self.half)

    def peer(self, distance):
        return self.base + lax.rem(self.own + distance, self.half)


def core_kernel(
    size,
    gain_hbm,
    bounds_hbm,
    live_hbm,
    features_hbm,
    stem_hbm,
    mid_dw_hbm,
    mid_w_hbm,
    last_dw_hbm,
    last_w_hbm,
    cot_hbm,
    proj_hbm,
    qkv_hbm,
    out_hbm,
    block_out_hbm,
    frame_grads_hbm,
    proj_grads_hbm,
    block_out_ref,
    frame_grads_ref,
    proj_grads_ref,
    gain_ref,
    bounds_ref,
    live_ref,
    stem_w,
    mid_dw,
    mid_w,
    last_dw,
    last_w,
    turned_features,
    feature_rows,
    x_own,
    halo_out,
    halo_in,
    flat_ref,
    turned_ref,
    even,
    odd_part,
    second,
    shifted,
    taps,
    cot_ref,
    proj_w,
    qkv_w,
    out_w,
    xw,
    do_ref,
    pj,
    mixed_ref,
    grads_ref,
    bias_ref,
    stat_ref,
    normalized_ref,
    panels,
    columns,
    out_part,
    in_part,
    load_sem,
    halo_sem,
    cot_send,
    cot_recv,
    send,
    recv,
    stat_send,
    stat_recv,
    col_send,
    col_recv,
    panel_send,
    panel_recv,
    part_send,
    part_recv,
    out_sem,
):
    rows, width = block_out_ref.shape
    window = (2 * REACH + 1) * rows
    depth = flat_ref.shape[1]
    share = depth // size
    count = width // PANEL
    me = lax.axis_index("tm")
    half = Half(size)
    cot_exchange = Exchange(size, cot_ref, cot_send, cot_recv)
    exchange = Exchange(size, xw, send, recv)
    odd = exchange.odd
    offsets = [o for o in range(-REACH, REACH + 1) if o]
    conv = Subsample(
        x_own, stem_w, mid_dw, mid_w, last_dw, last_w, flat_ref, turned_ref, even, odd_part, second, shifted, taps
    )

    def load(i, source, target):
        return pltpu.make_async_copy(source, target, load_sem.at[i])

    small = [
        load(0, cot_hbm, cot_ref.at[REACH]),
        load(1, stem_hbm, stem_w),
        load(2, mid_dw_hbm, mid_dw),
        load(3, mid_w_hbm, mid_w),
        load(4, last_dw_hbm, last_dw),
        load(5, last_w_hbm, last_w),
        load(10, gain_hbm, gain_ref),
        load(11, bounds_hbm, bounds_ref),
        load(12, live_hbm, live_ref),
    ]
    series = load(9, features_hbm, turned_features)
    series.start()
    large = [load(6, proj_hbm, proj_w), load(7, out_hbm, out_w), load(8, qkv_hbm, qkv_w)]
    for item in small:
        item.start()

    barrier = pltpu.get_barrier_semaphore()
    peers = 0
    for distance in range(1, size):
        other = lax.rem(me + distance, size)
        gap = other - me
        near = jnp.logical_and(gap >= -4, gap <= 4)
        same = other // half.half == me // half.half
        known = jnp.logical_or(jnp.logical_or(near, same), other == half.partner)
        peers += jnp.where(known, 1, 0)

        @pl.when(known)
        def _(other=other):
            pl.semaphore_signal(barrier, inc=1, device_id={"tm": other}, device_id_type=MESH)

    def there(offset):
        return jnp.logical_and(me + offset >= 0, me + offset < size)

    def when_there(offset, action):
        pl.when(there(offset))(lambda: action(offset))

    for offset in offsets:

        @pl.when(jnp.logical_not(there(offset)))
        def _(offset=offset):
            stat_ref[REACH + offset] = jnp.zeros(stat_ref.shape[1:], jnp.float32)

    slab = conv.rows
    conv.blank()
    series.wait()
    mel, times = turned_features.shape
    tall = jnp.concatenate(
        [turned_features[...].astype(jnp.float32), jnp.zeros((128 - mel, times), jnp.float32)], axis=0
    )
    feature_rows[...] = tall.T
    phases = [feature_rows[pl.ds(i, rows, stride=8), :] for i in range(8)]
    first_row = lax.broadcasted_iota(jnp.int32, (rows, 128), 0) == 0
    before = jnp.where(first_row, 0.0, pltpu.roll(phases[7], 1, 0))
    empty = jnp.zeros((rows, 128), jnp.float32)

    def lanes_at(part, dt):
        return pltpu.roll(jnp.concatenate([part, empty], axis=1), dt * MEL_PITCH + 1, 1)

    slabs = []
    for p in range(4):
        parts = [before if p == 0 else phases[2 * p - 1], phases[2 * p], phases[2 * p + 1]]
        built = sum(lanes_at(part, dt) for dt, part in enumerate(parts))
        tail = built[rows - 8 : rows]
        halo_out[8 * p : 8 * p + 8, :] = tail
        if p == 3:
            halo_out[32:40, :] = pltpu.roll(tail, 256 - 2 * MEL_PITCH, 1)
        slabs += [jnp.zeros((8, 256), jnp.float32), built]
    x_own[...] = jnp.concatenate(slabs, axis=0).astype(jnp.bfloat16)

    @pl.when(me == 0)
    def _():
        halo_in[...] = jnp.zeros(halo_in.shape, jnp.float32)

    def halo(target):
        return pltpu.make_async_remote_copy(
            src_ref=halo_out,
            dst_ref=halo_in,
            send_sem=halo_sem.at[0],
            recv_sem=halo_sem.at[1],
            device_id={"tm": target},
            device_id_type=MESH,
        )

    small[0].wait()
    pl.semaphore_wait(barrier, peers)
    pl.when(me + 1 < size)(lambda: halo(me + 1).start())
    cot_exchange.start()
    for item in large:
        item.start()
    for item in small[1:]:
        item.wait()
    conv.spread()
    cot_exchange.blank()
    exchange.blank()
    pl.when(me > 0)(lambda: halo(me - 1).wait_recv())
    place = lax.broadcasted_iota(jnp.int32, (8, 256), 0)
    lane = lax.broadcasted_iota(jnp.int32, (8, 256), 1)
    for p in range(4):
        top = x_own[p * slab : p * slab + 16, :].astype(jnp.float32)
        upper = jnp.where(place == 7, halo_in[8 * p : 8 * p + 8, :], top[0:8])
        lower = top[8:16]
        if p == 0:
            carried = jnp.broadcast_to(halo_in[39:40, :], (8, 256))
            lower = jnp.where((place == 0) & (lane < MEL_PITCH), carried, lower)
        x_own[p * slab : p * slab + 16, :] = jnp.concatenate([upper, lower], axis=0).astype(jnp.bfloat16)

    turns = conv.mids // 2
    marks = [turns * (i + 2) // (PIECES + 2) for i in range(PIECES + 1)]
    done = 0
    for j in range(PIECES):
        conv.run(done, marks[j])
        done = marks[j]
        cot_exchange.relay(j)
    conv.run(done, turns)
    for f in range(turns):
        conv.finish(f)
        if f >= 2 and f - 2 < PIECES:
            cot_exchange.relay_deep(f - 2)

    large[0].wait()
    frames = dot_nn(flat_ref[...], proj_w[...]).astype(jnp.bfloat16)
    frames_f = frames.astype(jnp.float32)
    centered = frames_f - jnp.mean(frames_f, axis=-1, keepdims=True)
    inv_std = lax.rsqrt(jnp.mean(centered * centered, axis=-1, keepdims=True) + norm_eps)
    normalized = centered * inv_std
    normalized_ref[...] = normalized
    block_out_ref[...] = frames
    xw[REACH] = (normalized * gain_ref[...]).astype(jnp.bfloat16)
    exchange.start()
    large[1].wait()
    cot_exchange.near_done()
    cot_exchange.deep_done()
    cot_exchange.twin().wait_recv()
    pl.when(cot_exchange.has_far)(lambda: cot_exchange.remote().wait_recv())
    cots = cot_ref[...].reshape(window, width)

    def d_attention(first, last):
        for i in range(first, last, 256):
            do_ref[:, i : i + 256] = dot_nt(cots, out_w[i : i + 256, :]).astype(jnp.bfloat16)

    first = (me - REACH) * rows
    own_col = segments(me * rows + lax.broadcasted_iota(jnp.int32, (rows, 128), 0), bounds_ref)
    for b in range(2 * REACH + 1):
        place = first + b * rows
        live = live_ref[0, b] == 1
        row = segments(place + lax.broadcasted_iota(jnp.int32, (8, rows), 1), bounds_ref)[0:1]
        same = (own_col[:, 0:1] == row) & live
        bias_ref[:, b * rows : (b + 1) * rows] = jnp.where(same, 0.0, neg_fill)

    def turned(target):
        start = pl.multiple_of(target * share, 16)
        return turned_ref.at[pl.ds(start, share), :]

    def landing(which, slot):
        start = pl.multiple_of(slot * rows, rows)
        return columns.at[pl.ds(which * share, share), pl.ds(start, rows)]

    def column(which, distance):
        target = half.peer(distance)
        other = target if which == 0 else lax.rem(target + half.half, size)
        return pltpu.make_async_remote_copy(
            src_ref=turned(other),
            dst_ref=landing(which, half.own),
            send_sem=col_send.at[which, distance],
            recv_sem=col_recv.at[which, distance],
            device_id={"tm": target},
            device_id_type=MESH,
        )

    def column_in(which, distance):
        slot = lax.rem(half.own - distance + half.half, half.half)
        return pltpu.make_async_remote_copy(
            src_ref=turned(me),
            dst_ref=landing(which, slot),
            send_sem=col_send.at[which, distance],
            recv_sem=col_recv.at[which, distance],
            device_id={"tm": half.peer(distance)},
            device_id_type=MESH,
        )

    def column_own(which):
        other = me if which == 0 else half.partner
        return pltpu.make_async_copy(turned(other), landing(which, half.own), col_send.at[which, 0])

    large[2].wait()

    def project(slot, blocks, first, last):
        x = xw[pl.ds(slot, blocks)].reshape(blocks * rows, width)
        for i in range(first, last, 512):
            out = dot_nn(x, qkv_w[:, i : i + 512]).astype(jnp.bfloat16)
            start = pl.multiple_of(slot * rows, rows)
            pj[pl.ds(start, blocks * rows), i : i + 512] = out

    d_attention(0, width // 2)
    exchange.relay(0)
    exchange.twin().wait_recv()
    project(REACH - odd, 2, 0, 3 * width // 2)
    exchange.relay(1)
    project(REACH - odd, 2, 3 * width // 2, 3 * width)
    exchange.relay(2)
    exchange.relay_deep(0)
    d_attention(width // 2, width)
    exchange.relay(3)
    exchange.relay_deep(1)
    for which in range(0, 1):
        column_own(which).start()
        for distance in range(1, half.half):
            column(which, distance).start()
    near_slot = (1 - odd) * exchange.upper + (5 - odd) * (1 - exchange.upper)
    deep_slot = (5 - odd) * exchange.upper + (1 - odd) * (1 - exchange.upper)
    pl.when(exchange.has_far)(lambda: exchange.remote().wait_recv())
    project(6 * odd, 1, 0, 3 * width)
    exchange.near_done()
    exchange.relay_deep(2)
    project(near_slot, 2, 0, 3 * width // 2)
    exchange.relay_deep(3)
    project(near_slot, 2, 3 * width // 2, 3 * width)
    exchange.deep_done()
    project(deep_slot, 2, 0, 3 * width)

    own = slice(REACH * rows, (REACH + 1) * rows)
    lanes = lax.broadcasted_iota(jnp.int32, (rows, 128), 1)

    def head(group, h):
        return pl.ds(pl.multiple_of(group * width + h * HEAD_DIM, HEAD_DIM), HEAD_DIM)

    def forward(h, stats):
        keys = pj[:, head(1, h)]
        values = pj[:, head(2, h)]
        scores = dot_nt(pj[own, head(0, h)], keys) * SCALE + bias_ref[...]
        dprob = dot_nt(do_ref[own, head(0, h)], values)
        top = jnp.max(scores, axis=1, keepdims=True)
        weights = jnp.exp(scores - top)
        mass = jnp.sum(weights, axis=1, keepdims=True)
        probs = weights * (1.0 / mass)
        delta = jnp.sum(probs * dprob, axis=1, keepdims=True)
        dscore = (probs * (dprob - delta)).astype(jnp.bfloat16)
        mixed_ref[:, head(0, h)] = dot_nn(probs.astype(jnp.bfloat16), values).astype(jnp.bfloat16)
        grads_ref[:, head(0, h)] = (dot_nn(dscore, keys) * SCALE).astype(jnp.bfloat16)
        stats = jnp.where(lanes == h, top + jnp.log(mass), stats)
        return jnp.where(lanes == HEADS + h, delta, stats)

    stats = lax.fori_loop(0, HEADS, forward, jnp.zeros((rows, 128), jnp.float32), unroll=4)
    stat_ref[REACH] = stats.T[0 : 2 * HEADS, :]

    def stat_copy(offset, slot, sem):
        return pltpu.make_async_remote_copy(
            src_ref=stat_ref.at[REACH],
            dst_ref=stat_ref.at[slot],
            send_sem=stat_send.at[REACH + offset],
            recv_sem=stat_recv.at[sem],
            device_id={"tm": me + offset},
            device_id_type=MESH,
        )

    def stat_out(offset):
        return stat_copy(offset, REACH - offset, REACH - offset)

    def stat_in(offset):
        return stat_copy(offset, REACH + offset, REACH + offset)

    for offset in offsets:
        when_there(offset, lambda o: stat_out(o).start())
    block_out_ref[...] = (
        block_out_ref[...].astype(jnp.float32) + dot_nn(mixed_ref[...], out_w[...])
    ).astype(jnp.bfloat16)
    stores = [
        pltpu.make_async_copy(block_out_ref, block_out_hbm, out_sem.at[0]),
        pltpu.make_async_copy(frame_grads_ref, frame_grads_hbm, out_sem.at[1]),
        pltpu.make_async_copy(proj_grads_ref, proj_grads_hbm, out_sem.at[2]),
    ]
    stores[0].start()
    grad_normed = dot_nt(grads_ref[:, 0:width], qkv_w[:, 0:width])
    for offset in offsets:
        when_there(offset, lambda o: stat_in(o).wait_recv())

    for which in range(1, 2):
        column_own(which).start()
        for distance in range(1, half.half):
            column(which, distance).start()

    def key_pass(h, _):
        queries = pj[:, head(0, h)]
        douts = do_ref[:, head(0, h)]
        blocks = range(2 * REACH + 1)
        log_norms = jnp.concatenate([stat_ref[b, pl.ds(h, 1), :] for b in blocks], axis=1)
        deltas = jnp.concatenate([stat_ref[b, pl.ds(HEADS + h, 1), :] for b in blocks], axis=1)
        scores = dot_nt(pj[own, head(1, h)], queries) * SCALE + bias_ref[...]
        dprob = dot_nt(pj[own, head(2, h)], douts)
        weights = jnp.exp(scores - log_norms)
        dscore = (weights * (dprob - deltas)).astype(jnp.bfloat16)
        grads_ref[:, head(1, h)] = (dot_nn(dscore, queries) * SCALE).astype(jnp.bfloat16)
        grads_ref[:, head(2, h)] = dot_nn(weights.astype(jnp.bfloat16), douts).astype(jnp.bfloat16)
        return 0

    lax.fori_loop(0, HEADS, key_pass, 0, unroll=4)
    grad_normed += dot_nt(grads_ref[:, width:], qkv_w[:, width:])
    normalized = normalized_ref[...]
    scaled = grad_normed * gain_ref[...]
    ln_grad = inv_std * (
        scaled
        - jnp.mean(scaled, axis=-1, keepdims=True)
        - normalized * jnp.mean(scaled * normalized, axis=-1, keepdims=True)
    )
    frame_grads = (cot_ref[REACH].astype(jnp.float32) + ln_grad).astype(jnp.bfloat16)
    for p in range(count):
        panels[p, half.own] = frame_grads[:, p * PANEL : (p + 1) * PANEL]

    def panel(p, slot, sem, target):
        return pltpu.make_async_remote_copy(
            src_ref=panels.at[p, slot],
            dst_ref=panels.at[p, slot],
            send_sem=panel_send.at[p, sem],
            recv_sem=panel_recv.at[p, sem],
            device_id={"tm": target},
            device_id_type=MESH,
        )

    steps = half.steps
    flip = half.across - half.me
    twin = half.sibling - half.me

    def along(p, s):
        return panel(p, half.own, s, half.base + half.turn(half.own, s))

    def along_in(p, s):
        return panel(p, half.turn(half.own, steps - s), s, half.base + half.turn(half.own, s))

    def cross(p, s):
        return panel(p, half.turn(half.own, steps - s), steps + s, half.across)

    def corner(p, s):
        return panel(p, half.own, steps + s, half.base + half.turn(half.own, s) + flip)

    def cross_in(p, s):
        return panel(p, half.turn(half.own, steps - s) + flip, steps + s, half.across)

    def twin_near(p, s):
        return panel(p, half.turn(half.own, steps - s), 2 * steps + s, half.sibling)

    def twin_near_in(p, s):
        return panel(p, half.turn(half.own, steps - s) + twin, 2 * steps + s, half.sibling)

    def twin_far(p, s):
        return panel(p, half.turn(half.own, steps - s) + flip, 3 * steps + s, half.sibling)

    def twin_far_in(p, s):
        return panel(p, half.turn(half.own, steps - s) + flip + twin, 3 * steps + s, half.sibling)

    def part(p):
        return pltpu.make_async_remote_copy(
            src_ref=out_part.at[p],
            dst_ref=in_part.at[p],
            send_sem=part_send.at[p],
            recv_sem=part_recv.at[p],
            device_id={"tm": half.partner},
            device_id_type=MESH,
        )

    def relay(p):
        for s in range(1, steps):
            along_in(p, s).wait_recv()
            if p >= DIRECT:
                cross(p, s).start()
            twin_near(p, s).start()

    def share_far(p):
        for s in range(steps):
            cross_in(p, s).wait_recv()
            twin_far(p, s).start()

    def multiply(p):
        for s in range(steps):
            twin_near_in(p, s).wait_recv()
            twin_far_in(p, s).wait_recv()
        sums = dot_nn(columns[...], panels[p].reshape(half.half * rows, PANEL))
        out_part[p] = sums[share:].astype(jnp.bfloat16)
        part(p).start()
        proj_grads_ref[:, p * PANEL : (p + 1) * PANEL] = sums[:share]

    for p in range(count):
        for s in range(1, steps):
            along(p, s).start()
            if p < DIRECT:
                corner(p, s).start()
        if p < AHEAD:
            cross(p, 0).start()
        twin_near(p, 0).start()
    frame_grads_ref[...] = frame_grads
    stores[1].start()
    for which in range(2):
        column_own(which).wait()
        for distance in range(1, half.half):
            column_in(which, distance).wait_recv()
    for t in range(count + 2):
        if t < count:
            relay(t)
            if t + AHEAD < count:
                cross(t + AHEAD, 0).start()
        if 1 <= t <= count:
            share_far(t - 1)
        if t >= 2:
            multiply(t - 2)
    for p in range(count):
        part(p).wait_recv()
        span = slice(p * PANEL, (p + 1) * PANEL)
        proj_grads_ref[:, span] = proj_grads_ref[:, span] + in_part[p].astype(jnp.float32)

    stores[2].start()
    cot_exchange.drain()
    exchange.drain()
    pl.when(me + 1 < size)(lambda: halo(me + 1).wait_send())
    for offset in offsets:
        when_there(offset, lambda o: stat_out(o).wait_send())
    for which in range(2):
        for distance in range(1, half.half):
            column(which, distance).wait_send()
    for p in range(count):
        for s in range(1, steps):
            along(p, s).wait_send()
            if p < DIRECT:
                corner(p, s).wait_send()
        for s in range(steps):
            if p >= DIRECT or s == 0:
                cross(p, s).wait_send()
            twin_near(p, s).wait_send()
            twin_far(p, s).wait_send()
        part(p).wait_send()
    for store in stores:
        store.wait()


def finish_kernel(a_ref, b_ref, c_ref, a_out, b_out, c_out, a_held, b_held, c_held, sem):
    held = (a_held, b_held, c_held)
    reads = [pltpu.make_async_copy(r, h, sem.at[i]) for i, (r, h) in enumerate(zip((a_ref, b_ref, c_ref), held))]
    writes = [pltpu.make_async_copy(h, o, sem.at[3 + i]) for i, (h, o) in enumerate(zip(held, (a_out, b_out, c_out)))]
    for item in reads:
        item.start()
    for read, write in zip(reads, writes):
        read.wait()
        write.start()
    for item in writes:
        item.wait()


def finished(arrays):
    hbm = pl.BlockSpec(memory_space=pl.ANY)
    return pl.pallas_call(
        finish_kernel,
        out_shape=tuple(jax.ShapeDtypeStruct(a.shape, a.dtype) for a in arrays),
        in_specs=[hbm] * 3,
        out_specs=(hbm,) * 3,
        scratch_shapes=[pltpu.VMEM(a.shape, a.dtype) for a in arrays] + [pltpu.SemaphoreType.DMA((6,))],
        name="finish",
    )(*arrays)


def core(
    size,
    features,
    gain,
    bounds,
    live,
    stem_kernel,
    mid_depthwise,
    mid_pointwise,
    last_depthwise,
    last_pointwise,
    cotangent,
    proj_weight,
    qkv_weight,
    out_weight,
):
    rows = cotangent.shape[0]
    slab = rows + 8
    mel = features.shape[0]
    mids = mel // 4
    channels = stem_kernel.shape[-1]
    depth, width = proj_weight.shape
    share = depth // size
    half = size // 2
    steps = half // 4
    count = width // PANEL
    blocks = 2 * REACH + 1
    hbm = pl.BlockSpec(memory_space=pl.ANY)
    dma = pltpu.SemaphoreType.DMA
    bf16, f32 = jnp.bfloat16, jnp.float32
    return pl.pallas_call(
        functools.partial(core_kernel, size),
        out_shape=(
            jax.ShapeDtypeStruct((rows, width), bf16),
            jax.ShapeDtypeStruct((rows, width), bf16),
            jax.ShapeDtypeStruct((share, width), f32),
        ),
        in_specs=[hbm] * 13,
        out_specs=(hbm,) * 3,
        scratch_shapes=[
            pltpu.VMEM((rows, width), bf16),
            pltpu.VMEM((rows, width), bf16),
            pltpu.VMEM((share, width), f32),
            pltpu.VMEM(gain.shape, f32),
            pltpu.SMEM(bounds.shape, jnp.int32),
            pltpu.SMEM(live.shape, jnp.int32),
            pltpu.VMEM(stem_kernel.shape, bf16),
            pltpu.VMEM(mid_depthwise.shape, bf16),
            pltpu.VMEM(mid_pointwise.shape, bf16),
            pltpu.VMEM(last_depthwise.shape, bf16),
            pltpu.VMEM(last_pointwise.shape, bf16),
            pltpu.VMEM(features.shape, bf16),
            pltpu.VMEM((features.shape[1], 128), f32),
            pltpu.VMEM((4 * slab, 256), bf16),
            pltpu.VMEM((40, 256), f32),
            pltpu.VMEM((40, 256), f32),
            pltpu.VMEM((rows, depth), bf16),
            pltpu.VMEM((depth, rows), bf16),
            pltpu.VMEM((4, slab, channels), f32),
            pltpu.VMEM((2, 4, slab, channels), f32),
            pltpu.VMEM((mids + 1, 2, slab, channels), f32),
            pltpu.VMEM((4, mel + 256, channels), f32),
            pltpu.VMEM((32, channels), f32),
            pltpu.VMEM((blocks, rows, width), bf16),
            pltpu.VMEM(proj_weight.shape, bf16),
            pltpu.VMEM(qkv_weight.shape, bf16),
            pltpu.VMEM(out_weight.shape, bf16),
            pltpu.VMEM((blocks, rows, width), bf16),
            pltpu.VMEM((blocks * rows, width), bf16),
            pltpu.VMEM((blocks * rows, 3 * width), bf16),
            pltpu.VMEM((rows, width), bf16),
            pltpu.VMEM((rows, 3 * width), bf16),
            pltpu.VMEM((rows, blocks * rows), f32),
            pltpu.VMEM((blocks, 2 * HEADS, rows), f32),
            pltpu.VMEM((rows, width), f32),
            pltpu.VMEM((count, half, rows, PANEL), bf16),
            pltpu.VMEM((2 * share, half * rows), bf16),
            pltpu.VMEM((count, share, PANEL), bf16),
            pltpu.VMEM((count, share, PANEL), bf16),
            dma((13,)),
            dma((2,)),
            dma((2 + 4 * PIECES,)),
            dma((2 + 4 * PIECES,)),
            dma((2 + 4 * PIECES,)),
            dma((2 + 4 * PIECES,)),
            dma((blocks,)),
            dma((blocks,)),
            dma((2, half)),
            dma((2, half)),
            dma((count, 4 * steps)),
            dma((count, 4 * steps)),
            dma((count,)),
            dma((count,)),
            dma((3,)),
        ],
        compiler_params=pltpu.CompilerParams(
            vmem_limit_bytes=58 * 1024 * 1024, collective_id=1, has_side_effects=True
        ),
        name="core",
    )(
        gain,
        bounds,
        live,
        features,
        stem_kernel,
        mid_depthwise,
        mid_pointwise,
        last_depthwise,
        last_pointwise,
        cotangent,
        proj_weight,
        qkv_weight,
        out_weight,
    )


def per_device(
    size,
    features,
    stem_kernel,
    mid_depthwise,
    mid_pointwise,
    last_depthwise,
    last_pointwise,
    proj_weight,
    norm_gain,
    qkv_weight,
    out_weight,
    cotangent,
    utt_bounds,
    live_blocks,
):
    results = core(
        size,
        features.T,
        norm_gain.reshape(1, -1),
        utt_bounds.T,
        live_blocks,
        stem_kernel,
        mid_depthwise,
        mid_pointwise,
        last_depthwise,
        last_pointwise,
        cotangent,
        proj_weight,
        qkv_weight,
        out_weight,
    )
    return finished(results)


def solution(mesh):
    split = P(("groups", "tm"), None)
    in_specs = (split,) + (P(),) * 9 + (split, P("groups", None), split)
    return jax.shard_map(
        functools.partial(per_device, mesh.shape["tm"]),
        mesh=mesh,
        in_specs=in_specs,
        out_specs=(split, split, split),
        check_vma=False,
    )
```

```python
import functools

import jax
import jax.numpy as jnp
from jax import lax
from jax.experimental import pallas as pl
from jax.experimental.pallas import tpu as pltpu
from jax.sharding import PartitionSpec as P

HEADS = 8
REACH = 3
HEAD_DIM = 128
norm_eps = 1e-05
neg_fill = -1e30
MEL_PITCH = 84
SCALE = HEAD_DIM ** (-0.5)
PIECES = 4
PANEL = 128
AHEAD = 4
DIRECT = 4


def dot_nt(a, b):
    return lax.dot_general(a, b, (((1,), (1,)), ((), ())), preferred_element_type=jnp.float32)


def dot_tn(a, b):
    return lax.dot_general(a, b, (((0,), (0,)), ((), ())), preferred_element_type=jnp.float32)


def dot_nn(a, b):
    return jnp.dot(a, b, preferred_element_type=jnp.float32)


MESH = pl.DeviceIdType.MESH


class Exchange:
    def __init__(self, size, out_ref, send, recv):
        self.size, self.out, self.send, self.recv = size, out_ref, send, recv
        self.rows = out_ref.shape[1] // PIECES
        self.me = lax.axis_index("tm")
        self.odd = lax.rem(self.me, 2)
        self.upper = lax.rem(self.me // 2, 2)
        self.sibling = self.me + 1 - 2 * self.odd
        self.beside = self.me + 2 - 4 * self.upper
        self.far = self.me - 3 + 6 * self.odd
        self.onward = self.me + 4 - 8 * self.upper
        self.back = self.me - 4 + 8 * self.upper
        self.has_far = self.inside(self.far)
        self.has_onward = self.inside(self.onward)
        self.has_back = self.inside(self.back)
        self.low = 1 + 4 * self.upper
        self.high = 5 - 4 * self.upper

    def inside(self, target):
        return jnp.logical_and(target >= 0, target < self.size)

    def copy(self, source, slot, sem, target):
        return pltpu.make_async_remote_copy(
            src_ref=self.out.at[source],
            dst_ref=self.out.at[slot],
            send_sem=self.send.at[sem],
            recv_sem=self.recv.at[sem],
            device_id={"tm": target},
            device_id_type=MESH,
        )

    def piece(self, source, slot, sem, target, j):
        span = pl.ds(j * self.rows, self.rows)
        return pltpu.make_async_remote_copy(
            src_ref=self.out.at[source, span, :],
            dst_ref=self.out.at[slot, span, :],
            send_sem=self.send.at[sem],
            recv_sem=self.recv.at[sem],
            device_id={"tm": target},
            device_id_type=MESH,
        )

    def twin(self):
        return self.copy(REACH, 2 + 2 * self.odd, 0, self.sibling)

    def remote(self):
        return self.copy(REACH, 6 - 6 * self.odd, 1, self.far)

    def near(self, j):
        return self.piece(REACH, self.low, 2 + j, self.beside, j)

    def near_in(self, j):
        return self.piece(REACH, self.high, 2 + j, self.beside, j)

    def deep(self, j):
        return self.piece(self.high, self.low, 2 + PIECES + j, self.onward, j)

    def deep_in(self, j):
        return self.piece(REACH, self.low, 2 + PIECES + j, self.back, j)

    def near_pass(self, j):
        slot = 4 - 4 * self.upper + 2 * self.odd
        return self.piece(self.high, slot, 2 + 2 * PIECES + j, self.sibling, j)

    def near_pass_in(self, j):
        slot = 6 - 4 * self.upper - 2 * self.odd
        return self.piece(REACH, slot, 2 + 2 * PIECES + j, self.sibling, j)

    def deep_pass(self, j):
        slot = 4 * self.upper + 2 * self.odd
        return self.piece(self.low, slot, 2 + 3 * PIECES + j, self.sibling, j)

    def deep_pass_in(self, j):
        slot = 4 * self.upper + 2 - 2 * self.odd
        return self.piece(REACH, slot, 2 + 3 * PIECES + j, self.sibling, j)

    def blank(self):
        for slot in range(2 * REACH + 1):
            if slot != REACH:

                @pl.when(jnp.logical_not(self.inside(self.me + slot - REACH)))
                def _(slot=slot):
                    self.out[slot] = jnp.zeros(self.out.shape[1:], self.out.dtype)

    def start(self):
        for j in range(PIECES):
            self.near(j).start()
        pl.when(self.has_far)(lambda: self.remote().start())
        self.twin().start()

    def relay(self, j):
        self.near_in(j).wait_recv()
        pl.when(self.has_onward)(lambda: self.deep(j).start())
        self.near_pass(j).start()

    def relay_deep(self, j):
        @pl.when(self.has_back)
        def _():
            self.deep_in(j).wait_recv()
            self.deep_pass(j).start()

    def near_done(self):
        for j in range(PIECES):
            self.near_pass_in(j).wait_recv()

    def deep_done(self):
        for j in range(PIECES):
            pl.when(self.has_back)(lambda: self.deep_pass_in(j).wait_recv())

    def drain(self):
        self.twin().wait_send()
        pl.when(self.has_far)(lambda: self.remote().wait_send())
        for j in range(PIECES):
            self.near(j).wait_send()
            self.near_pass(j).wait_send()
            pl.when(self.has_onward)(lambda: self.deep(j).wait_send())
            pl.when(self.has_back)(lambda: self.deep_pass(j).wait_send())


def segments(positions, bounds_ref):
    found = jnp.zeros(positions.shape, jnp.int32)
    for u in range(bounds_ref.shape[1]):
        inside = (positions >= bounds_ref[0, u]) & (positions < bounds_ref[1, u])
        found = jnp.where(inside, u + 1, found)
    return found


class Subsample:
    def __init__(self, x, stem_w, mid_dw, mid_w, last_dw, last_w, flat, turned, even, odd, second, shifted, taps):
        self.x, self.stem_w, self.mid_dw, self.mid_w = x, stem_w, mid_dw, mid_w
        self.last_dw, self.last_w, self.flat, self.turned = last_dw, last_w, flat, turned
        self.even, self.odd, self.second, self.shifted, self.taps = even, odd, second, shifted, taps
        self.rows = x.shape[0] // 4
        self.main = self.rows - 8
        self.mids = second.shape[0] - 1
        self.span = shifted.shape[1] - 256

    def blank(self):
        self.odd[0] = jnp.zeros(self.odd.shape[1:], self.odd.dtype)
        self.second[0] = jnp.zeros(self.second.shape[1:], self.second.dtype)
        self.shifted[...] = jnp.zeros(self.shifted.shape, jnp.float32)

    def spread(self):
        for dt in range(3):
            for df in range(3):
                row = 3 * dt + df
                tap = self.stem_w[dt, df : df + 1, :].astype(jnp.float32)
                for i in range(4):
                    at = self.span + 2 * i + dt * MEL_PITCH + df
                    self.shifted[i, at : at + 1, :] = tap
                self.taps[row : row + 1, :] = self.mid_dw[dt, df : df + 1, :].astype(jnp.float32)
                last = self.last_dw[dt, df : df + 1, :].astype(jnp.float32)
                self.taps[16 + row : 17 + row, :] = last

    def step(self, k, half):
        main, rows, second = self.main, self.rows, self.second

        def stem(i):
            start = pl.multiple_of(self.span - 8 * k, 8)
            taps = self.shifted[i, pl.ds(start, 256), :].astype(jnp.bfloat16)
            return jnp.maximum(dot_nn(self.x[...], taps), 0.0).reshape(self.even.shape)

        m = 2 * k + half
        self.even[...] = stem(2 * half)
        self.odd[1 - half] = stem(2 * half + 1)
        parts = (self.odd.at[half], self.even, self.odd.at[1 - half])
        early = jnp.zeros((main, 256), jnp.float32)
        late = jnp.zeros((rows, 256), jnp.float32)
        for df in range(3):
            part = parts[df]
            for dt in range(3):
                tap = self.taps[3 * dt + df : 3 * dt + df + 1, :]
                phase = (3, 0, 1)[dt]
                start = 7 if dt == 0 else 8
                early += part[phase, start : start + main, :] * tap
                late += part[dt + 1] * tap
        weight = self.mid_w[...]
        second[m + 1, 0, 8:rows, :] = jnp.maximum(dot_nn(early.astype(jnp.bfloat16), weight), 0.0)
        second[m + 1, 1] = jnp.maximum(dot_nn(late.astype(jnp.bfloat16), weight), 0.0)

    def run(self, first, last):
        def body(k, _):
            self.step(k, 0)
            self.step(k, 1)
            return 0

        lax.fori_loop(first, last, body, 0, unroll=True)

    def finish(self, f):
        total = jnp.zeros((self.main, 256), jnp.float32)
        for df in range(3):
            for dt in range(3):
                tap = self.taps[16 + 3 * dt + df : 17 + 3 * dt + df, :]
                phase = (1, 0, 1)[dt]
                start = 7 if dt == 0 else 8
                total += self.second[2 * f + df, phase, start : start + self.main, :] * tap
        out = jnp.maximum(dot_nn(total.astype(jnp.bfloat16), self.last_w[...]), 0.0)
        self.flat[:, f * 256 : (f + 1) * 256] = out.astype(jnp.bfloat16)
        self.turned[f * 256 : (f + 1) * 256, :] = out.T.astype(jnp.bfloat16)


class Half:
    def __init__(self, size):
        self.size, self.half = size, size // 2
        self.me = lax.axis_index("tm")
        self.base = self.me // self.half * self.half
        self.own = self.me - self.base
        self.partner = self.half - self.base + self.own
        self.core = lax.rem(self.me, 2)
        self.sibling = self.me + 1 - 2 * self.core
        self.across = self.me + 2 - 4 * lax.rem(self.me // 2, 2)
        self.steps = self.half // 4

    def turn(self, slot, step):
        return lax.rem(slot + 4 * step, self.half)

    def peer(self, distance):
        return self.base + lax.rem(self.own + distance, self.half)


def core_kernel(
    size,
    gain_hbm,
    bounds_hbm,
    live_hbm,
    features_hbm,
    stem_hbm,
    mid_dw_hbm,
    mid_w_hbm,
    last_dw_hbm,
    last_w_hbm,
    cot_hbm,
    proj_hbm,
    qkv_hbm,
    out_hbm,
    block_out_hbm,
    frame_grads_hbm,
    proj_grads_hbm,
    block_out_ref,
    frame_grads_ref,
    proj_grads_ref,
    gain_ref,
    bounds_ref,
    live_ref,
    stem_w,
    mid_dw,
    mid_w,
    last_dw,
    last_w,
    turned_features,
    feature_rows,
    x_own,
    halo_out,
    halo_in,
    flat_ref,
    turned_ref,
    even,
    odd_part,
    second,
    shifted,
    taps,
    cot_ref,
    proj_w,
    qkv_w,
    out_w,
    xw,
    do_ref,
    pj,
    mixed_ref,
    grads_ref,
    bias_ref,
    stat_ref,
    normalized_ref,
    panels,
    columns,
    out_part,
    in_part,
    load_sem,
    halo_sem,
    cot_send,
    cot_recv,
    send,
    recv,
    stat_send,
    stat_recv,
    col_send,
    col_recv,
    panel_send,
    panel_recv,
    part_send,
    part_recv,
    out_sem,
):
    rows, width = block_out_ref.shape
    window = (2 * REACH + 1) * rows
    depth = flat_ref.shape[1]
    share = depth // size
    count = width // PANEL
    me = lax.axis_index("tm")
    half = Half(size)
    cot_exchange = Exchange(size, cot_ref, cot_send, cot_recv)
    exchange = Exchange(size, xw, send, recv)
    odd = exchange.odd
    offsets = [o for o in range(-REACH, REACH + 1) if o]
    conv = Subsample(
        x_own, stem_w, mid_dw, mid_w, last_dw, last_w, flat_ref, turned_ref, even, odd_part, second, shifted, taps
    )

    def load(i, source, target):
        return pltpu.make_async_copy(source, target, load_sem.at[i])

    small = [
        load(0, cot_hbm, cot_ref.at[REACH]),
        load(1, stem_hbm, stem_w),
        load(2, mid_dw_hbm, mid_dw),
        load(3, mid_w_hbm, mid_w),
        load(4, last_dw_hbm, last_dw),
        load(5, last_w_hbm, last_w),
        load(10, gain_hbm, gain_ref),
        load(11, bounds_hbm, bounds_ref),
        load(12, live_hbm, live_ref),
    ]
    series = load(9, features_hbm, turned_features)
    series.start()
    large = [load(6, proj_hbm, proj_w), load(7, out_hbm, out_w), load(8, qkv_hbm, qkv_w)]
    for item in small:
        item.start()

    barrier = pltpu.get_barrier_semaphore()
    peers = 0
    for distance in range(1, size):
        other = lax.rem(me + distance, size)
        gap = other - me
        near = jnp.logical_and(gap >= -4, gap <= 4)
        same = other // half.half == me // half.half
        known = jnp.logical_or(jnp.logical_or(near, same), other == half.partner)
        peers += jnp.where(known, 1, 0)

        @pl.when(known)
        def _(other=other):
            pl.semaphore_signal(barrier, inc=1, device_id={"tm": other}, device_id_type=MESH)

    def there(offset):
        return jnp.logical_and(me + offset >= 0, me + offset < size)

    def when_there(offset, action):
        pl.when(there(offset))(lambda: action(offset))

    for offset in offsets:

        @pl.when(jnp.logical_not(there(offset)))
        def _(offset=offset):
            stat_ref[REACH + offset] = jnp.zeros(stat_ref.shape[1:], jnp.float32)

    slab = conv.rows
    conv.blank()
    series.wait()
    mel, times = turned_features.shape
    tall = jnp.concatenate(
        [turned_features[...].astype(jnp.float32), jnp.zeros((128 - mel, times), jnp.float32)], axis=0
    )
    feature_rows[...] = tall.T
    phases = [feature_rows[pl.ds(i, rows, stride=8), :] for i in range(8)]
    first_row = lax.broadcasted_iota(jnp.int32, (rows, 128), 0) == 0
    before = jnp.where(first_row, 0.0, pltpu.roll(phases[7], 1, 0))
    empty = jnp.zeros((rows, 128), jnp.float32)

    def lanes_at(part, dt):
        return pltpu.roll(jnp.concatenate([part, empty], axis=1), dt * MEL_PITCH + 1, 1)

    slabs = []
    for p in range(4):
        parts = [before if p == 0 else phases[2 * p - 1], phases[2 * p], phases[2 * p + 1]]
        built = sum(lanes_at(part, dt) for dt, part in enumerate(parts))
        tail = built[rows - 8 : rows]
        halo_out[8 * p : 8 * p + 8, :] = tail
        if p == 3:
            halo_out[32:40, :] = pltpu.roll(tail, 256 - 2 * MEL_PITCH, 1)
        slabs += [jnp.zeros((8, 256), jnp.float32), built]
    x_own[...] = jnp.concatenate(slabs, axis=0).astype(jnp.bfloat16)

    @pl.when(me == 0)
    def _():
        halo_in[...] = jnp.zeros(halo_in.shape, jnp.float32)

    def halo(target):
        return pltpu.make_async_remote_copy(
            src_ref=halo_out,
            dst_ref=halo_in,
            send_sem=halo_sem.at[0],
            recv_sem=halo_sem.at[1],
            device_id={"tm": target},
            device_id_type=MESH,
        )

    small[0].wait()
    pl.semaphore_wait(barrier, peers)
    pl.when(me + 1 < size)(lambda: halo(me + 1).start())
    cot_exchange.start()
    for item in large:
        item.start()
    for item in small[1:]:
        item.wait()
    conv.spread()
    cot_exchange.blank()
    exchange.blank()
    pl.when(me > 0)(lambda: halo(me - 1).wait_recv())
    place = lax.broadcasted_iota(jnp.int32, (8, 256), 0)
    lane = lax.broadcasted_iota(jnp.int32, (8, 256), 1)
    for p in range(4):
        top = x_own[p * slab : p * slab + 16, :].astype(jnp.float32)
        upper = jnp.where(place == 7, halo_in[8 * p : 8 * p + 8, :], top[0:8])
        lower = top[8:16]
        if p == 0:
            carried = jnp.broadcast_to(halo_in[39:40, :], (8, 256))
            lower = jnp.where((place == 0) & (lane < MEL_PITCH), carried, lower)
        x_own[p * slab : p * slab + 16, :] = jnp.concatenate([upper, lower], axis=0).astype(jnp.bfloat16)

    turns = conv.mids // 2
    marks = [turns * (i + 2) // (PIECES + 2) for i in range(PIECES + 1)]
    done = 0
    for j in range(PIECES):
        conv.run(done, marks[j])
        done = marks[j]
        cot_exchange.relay(j)
    conv.run(done, turns)
    for f in range(turns):
        conv.finish(f)
        if f >= 2 and f - 2 < PIECES:
            cot_exchange.relay_deep(f - 2)

    large[0].wait()
    frames = dot_nn(flat_ref[...], proj_w[...]).astype(jnp.bfloat16)
    frames_f = frames.astype(jnp.float32)
    centered = frames_f - jnp.mean(frames_f, axis=-1, keepdims=True)
    inv_std = lax.rsqrt(jnp.mean(centered * centered, axis=-1, keepdims=True) + norm_eps)
    normalized = centered * inv_std
    normalized_ref[...] = normalized
    block_out_ref[...] = frames
    xw[REACH] = (normalized * gain_ref[...]).astype(jnp.bfloat16)
    exchange.start()
    large[1].wait()
    cot_exchange.near_done()
    cot_exchange.deep_done()
    cot_exchange.twin().wait_recv()
    pl.when(cot_exchange.has_far)(lambda: cot_exchange.remote().wait_recv())
    cots = cot_ref[...].reshape(window, width)

    def d_attention(first, last):
        for i in range(first, last, 256):
            do_ref[:, i : i + 256] = dot_nt(cots, out_w[i : i + 256, :]).astype(jnp.bfloat16)

    first = (me - REACH) * rows
    own_col = segments(me * rows + lax.broadcasted_iota(jnp.int32, (rows, 128), 0), bounds_ref)
    for b in range(2 * REACH + 1):
        place = first + b * rows
        live = live_ref[0, b] == 1
        row = segments(place + lax.broadcasted_iota(jnp.int32, (8, rows), 1), bounds_ref)[0:1]
        same = (own_col[:, 0:1] == row) & live
        bias_ref[:, b * rows : (b + 1) * rows] = jnp.where(same, 0.0, neg_fill)

    def turned(target):
        start = pl.multiple_of(target * share, 16)
        return turned_ref.at[pl.ds(start, share), :]

    def landing(which, slot):
        start = pl.multiple_of(slot * rows, rows)
        return columns.at[pl.ds(which * share, share), pl.ds(start, rows)]

    def column(which, distance):
        target = half.peer(distance)
        other = target if which == 0 else lax.rem(target + half.half, size)
        return pltpu.make_async_remote_copy(
            src_ref=turned(other),
            dst_ref=landing(which, half.own),
            send_sem=col_send.at[which, distance],
            recv_sem=col_recv.at[which, distance],
            device_id={"tm": target},
            device_id_type=MESH,
        )

    def column_in(which, distance):
        slot = lax.rem(half.own - distance + half.half, half.half)
        return pltpu.make_async_remote_copy(
            src_ref=turned(me),
            dst_ref=landing(which, slot),
            send_sem=col_send.at[which, distance],
            recv_sem=col_recv.at[which, distance],
            device_id={"tm": half.peer(distance)},
            device_id_type=MESH,
        )

    def column_own(which):
        other = me if which == 0 else half.partner
        return pltpu.make_async_copy(turned(other), landing(which, half.own), col_send.at[which, 0])

    large[2].wait()

    def project(slot, blocks, first, last):
        x = xw[pl.ds(slot, blocks)].reshape(blocks * rows, width)
        for i in range(first, last, 512):
            out = dot_nn(x, qkv_w[:, i : i + 512]).astype(jnp.bfloat16)
            start = pl.multiple_of(slot * rows, rows)
            pj[pl.ds(start, blocks * rows), i : i + 512] = out

    d_attention(0, width // 2)
    exchange.relay(0)
    exchange.twin().wait_recv()
    project(REACH - odd, 2, 0, 3 * width // 2)
    exchange.relay(1)
    project(REACH - odd, 2, 3 * width // 2, 3 * width)
    exchange.relay(2)
    exchange.relay_deep(0)
    d_attention(width // 2, width)
    exchange.relay(3)
    exchange.relay_deep(1)
    for which in range(0, 1):
        column_own(which).start()
        for distance in range(1, half.half):
            column(which, distance).start()
    near_slot = (1 - odd) * exchange.upper + (5 - odd) * (1 - exchange.upper)
    deep_slot = (5 - odd) * exchange.upper + (1 - odd) * (1 - exchange.upper)
    pl.when(exchange.has_far)(lambda: exchange.remote().wait_recv())
    project(6 * odd, 1, 0, 3 * width)
    exchange.near_done()
    exchange.relay_deep(2)
    project(near_slot, 2, 0, 3 * width // 2)
    exchange.relay_deep(3)
    project(near_slot, 2, 3 * width // 2, 3 * width)
    exchange.deep_done()
    project(deep_slot, 2, 0, 3 * width)

    own = slice(REACH * rows, (REACH + 1) * rows)
    lanes = lax.broadcasted_iota(jnp.int32, (rows, 128), 1)

    def head(group, h):
        return pl.ds(pl.multiple_of(group * width + h * HEAD_DIM, HEAD_DIM), HEAD_DIM)

    def forward(h, stats):
        keys = pj[:, head(1, h)]
        values = pj[:, head(2, h)]
        scores = dot_nt(pj[own, head(0, h)], keys) * SCALE + bias_ref[...]
        dprob = dot_nt(do_ref[own, head(0, h)], values)
        top = jnp.max(scores, axis=1, keepdims=True)
        weights = jnp.exp(scores - top)
        mass = jnp.sum(weights, axis=1, keepdims=True)
        probs = weights * (1.0 / mass)
        delta = jnp.sum(probs * dprob, axis=1, keepdims=True)
        dscore = (probs * (dprob - delta)).astype(jnp.bfloat16)
        mixed_ref[:, head(0, h)] = dot_nn(probs.astype(jnp.bfloat16), values).astype(jnp.bfloat16)
        grads_ref[:, head(0, h)] = (dot_nn(dscore, keys) * SCALE).astype(jnp.bfloat16)
        stats = jnp.where(lanes == h, top + jnp.log(mass), stats)
        return jnp.where(lanes == HEADS + h, delta, stats)

    stats = lax.fori_loop(0, HEADS, forward, jnp.zeros((rows, 128), jnp.float32), unroll=8)
    stat_ref[REACH] = stats.T[0 : 2 * HEADS, :]

    def stat_copy(offset, slot, sem):
        return pltpu.make_async_remote_copy(
            src_ref=stat_ref.at[REACH],
            dst_ref=stat_ref.at[slot],
            send_sem=stat_send.at[REACH + offset],
            recv_sem=stat_recv.at[sem],
            device_id={"tm": me + offset},
            device_id_type=MESH,
        )

    def stat_out(offset):
        return stat_copy(offset, REACH - offset, REACH - offset)

    def stat_in(offset):
        return stat_copy(offset, REACH + offset, REACH + offset)

    for offset in offsets:
        when_there(offset, lambda o: stat_out(o).start())
    block_out_ref[...] = (
        block_out_ref[...].astype(jnp.float32) + dot_nn(mixed_ref[...], out_w[...])
    ).astype(jnp.bfloat16)
    stores = [
        pltpu.make_async_copy(block_out_ref, block_out_hbm, out_sem.at[0]),
        pltpu.make_async_copy(frame_grads_ref, frame_grads_hbm, out_sem.at[1]),
    ]
    for i in range(2):
        side = slice(i * width // 2, (i + 1) * width // 2)
        stores.append(
            pltpu.make_async_copy(proj_grads_ref.at[:, side], proj_grads_hbm.at[:, side], out_sem.at[2 + i])
        )
    stores[0].start()
    grad_normed = dot_nt(grads_ref[:, 0:width], qkv_w[:, 0:width])
    for offset in offsets:
        when_there(offset, lambda o: stat_in(o).wait_recv())

    for which in range(1, 2):
        column_own(which).start()
        for distance in range(1, half.half):
            column(which, distance).start()

    def key_pass(h, _):
        queries = pj[:, head(0, h)]
        douts = do_ref[:, head(0, h)]
        blocks = range(2 * REACH + 1)
        log_norms = jnp.concatenate([stat_ref[b, pl.ds(h, 1), :] for b in blocks], axis=1)
        deltas = jnp.concatenate([stat_ref[b, pl.ds(HEADS + h, 1), :] for b in blocks], axis=1)
        scores = dot_nt(pj[own, head(1, h)], queries) * SCALE + bias_ref[...]
        dprob = dot_nt(pj[own, head(2, h)], douts)
        weights = jnp.exp(scores - log_norms)
        dscore = (weights * (dprob - deltas)).astype(jnp.bfloat16)
        grads_ref[:, head(1, h)] = (dot_nn(dscore, queries) * SCALE).astype(jnp.bfloat16)
        grads_ref[:, head(2, h)] = dot_nn(weights.astype(jnp.bfloat16), douts).astype(jnp.bfloat16)
        return 0

    lax.fori_loop(0, HEADS, key_pass, 0, unroll=8)
    grad_normed += dot_nt(grads_ref[:, width:], qkv_w[:, width:])
    normalized = normalized_ref[...]
    scaled = grad_normed * gain_ref[...]
    ln_grad = inv_std * (
        scaled
        - jnp.mean(scaled, axis=-1, keepdims=True)
        - normalized * jnp.mean(scaled * normalized, axis=-1, keepdims=True)
    )
    frame_grads = (cot_ref[REACH].astype(jnp.float32) + ln_grad).astype(jnp.bfloat16)
    for p in range(count):
        panels[p, half.own] = frame_grads[:, p * PANEL : (p + 1) * PANEL]

    def panel(p, slot, sem, target):
        return pltpu.make_async_remote_copy(
            src_ref=panels.at[p, slot],
            dst_ref=panels.at[p, slot],
            send_sem=panel_send.at[p, sem],
            recv_sem=panel_recv.at[p, sem],
            device_id={"tm": target},
            device_id_type=MESH,
        )

    steps = half.steps
    flip = half.across - half.me
    twin = half.sibling - half.me

    def along(p, s):
        return panel(p, half.own, s, half.base + half.turn(half.own, s))

    def along_in(p, s):
        return panel(p, half.turn(half.own, steps - s), s, half.base + half.turn(half.own, s))

    def cross(p, s):
        return panel(p, half.turn(half.own, steps - s), steps + s, half.across)

    def corner(p, s):
        return panel(p, half.own, steps + s, half.base + half.turn(half.own, s) + flip)

    def cross_in(p, s):
        return panel(p, half.turn(half.own, steps - s) + flip, steps + s, half.across)

    def twin_near(p, s):
        return panel(p, half.turn(half.own, steps - s), 2 * steps + s, half.sibling)

    def twin_near_in(p, s):
        return panel(p, half.turn(half.own, steps - s) + twin, 2 * steps + s, half.sibling)

    def twin_far(p, s):
        return panel(p, half.turn(half.own, steps - s) + flip, 3 * steps + s, half.sibling)

    def twin_far_in(p, s):
        return panel(p, half.turn(half.own, steps - s) + flip + twin, 3 * steps + s, half.sibling)

    def part(p):
        return pltpu.make_async_remote_copy(
            src_ref=out_part.at[p],
            dst_ref=in_part.at[p],
            send_sem=part_send.at[p],
            recv_sem=part_recv.at[p],
            device_id={"tm": half.partner},
            device_id_type=MESH,
        )

    def relay(p):
        for s in range(1, steps):
            along_in(p, s).wait_recv()
            if p >= DIRECT:
                cross(p, s).start()
            twin_near(p, s).start()

    def share_far(p):
        for s in range(steps):
            cross_in(p, s).wait_recv()
            twin_far(p, s).start()

    def multiply(p):
        for s in range(steps):
            twin_near_in(p, s).wait_recv()
            twin_far_in(p, s).wait_recv()
        sums = dot_nn(columns[...], panels[p].reshape(half.half * rows, PANEL))
        out_part[p] = sums[share:].astype(jnp.bfloat16)
        part(p).start()
        proj_grads_ref[:, p * PANEL : (p + 1) * PANEL] = sums[:share]

    for p in range(count):
        for s in range(1, steps):
            along(p, s).start()
            if p < DIRECT:
                corner(p, s).start()
        if p < AHEAD:
            cross(p, 0).start()
        twin_near(p, 0).start()
    frame_grads_ref[...] = frame_grads
    stores[1].start()
    for which in range(2):
        column_own(which).wait()
        for distance in range(1, half.half):
            column_in(which, distance).wait_recv()
    for t in range(count + 2):
        if t < count:
            relay(t)
            if t + AHEAD < count:
                cross(t + AHEAD, 0).start()
        if 1 <= t <= count:
            share_far(t - 1)
        if t >= 2:
            multiply(t - 2)
    for p in range(count):
        part(p).wait_recv()
        span = slice(p * PANEL, (p + 1) * PANEL)
        proj_grads_ref[:, span] = proj_grads_ref[:, span] + in_part[p].astype(jnp.float32)
        if p + 1 == count // 2:
            stores[2].start()

    stores[3].start()
    cot_exchange.drain()
    exchange.drain()
    pl.when(me + 1 < size)(lambda: halo(me + 1).wait_send())
    for offset in offsets:
        when_there(offset, lambda o: stat_out(o).wait_send())
    for which in range(2):
        for distance in range(1, half.half):
            column(which, distance).wait_send()
    for p in range(count):
        for s in range(1, steps):
            along(p, s).wait_send()
            if p < DIRECT:
                corner(p, s).wait_send()
        for s in range(steps):
            if p >= DIRECT or s == 0:
                cross(p, s).wait_send()
            twin_near(p, s).wait_send()
            twin_far(p, s).wait_send()
        part(p).wait_send()
    for store in stores:
        store.wait()


def finish_kernel(a_ref, b_ref, c_ref, a_out, b_out, c_out, a_held, b_held, c_held, sem):
    held = (a_held, b_held, c_held)
    reads = [pltpu.make_async_copy(r, h, sem.at[i]) for i, (r, h) in enumerate(zip((a_ref, b_ref, c_ref), held))]
    writes = [pltpu.make_async_copy(h, o, sem.at[3 + i]) for i, (h, o) in enumerate(zip(held, (a_out, b_out, c_out)))]
    for item in reads:
        item.start()
    for read, write in zip(reads, writes):
        read.wait()
        write.start()
    for item in writes:
        item.wait()


def finished(arrays):
    hbm = pl.BlockSpec(memory_space=pl.ANY)
    return pl.pallas_call(
        finish_kernel,
        out_shape=tuple(jax.ShapeDtypeStruct(a.shape, a.dtype) for a in arrays),
        in_specs=[hbm] * 3,
        out_specs=(hbm,) * 3,
        scratch_shapes=[pltpu.VMEM(a.shape, a.dtype) for a in arrays] + [pltpu.SemaphoreType.DMA((6,))],
        name="finish",
    )(*arrays)


def core(
    size,
    features,
    gain,
    bounds,
    live,
    stem_kernel,
    mid_depthwise,
    mid_pointwise,
    last_depthwise,
    last_pointwise,
    cotangent,
    proj_weight,
    qkv_weight,
    out_weight,
):
    rows = cotangent.shape[0]
    slab = rows + 8
    mel = features.shape[0]
    mids = mel // 4
    channels = stem_kernel.shape[-1]
    depth, width = proj_weight.shape
    share = depth // size
    half = size // 2
    steps = half // 4
    count = width // PANEL
    blocks = 2 * REACH + 1
    hbm = pl.BlockSpec(memory_space=pl.ANY)
    dma = pltpu.SemaphoreType.DMA
    bf16, f32 = jnp.bfloat16, jnp.float32
    return pl.pallas_call(
        functools.partial(core_kernel, size),
        out_shape=(
            jax.ShapeDtypeStruct((rows, width), bf16),
            jax.ShapeDtypeStruct((rows, width), bf16),
            jax.ShapeDtypeStruct((share, width), f32),
        ),
        in_specs=[hbm] * 13,
        out_specs=(hbm,) * 3,
        scratch_shapes=[
            pltpu.VMEM((rows, width), bf16),
            pltpu.VMEM((rows, width), bf16),
            pltpu.VMEM((share, width), f32),
            pltpu.VMEM(gain.shape, f32),
            pltpu.SMEM(bounds.shape, jnp.int32),
            pltpu.SMEM(live.shape, jnp.int32),
            pltpu.VMEM(stem_kernel.shape, bf16),
            pltpu.VMEM(mid_depthwise.shape, bf16),
            pltpu.VMEM(mid_pointwise.shape, bf16),
            pltpu.VMEM(last_depthwise.shape, bf16),
            pltpu.VMEM(last_pointwise.shape, bf16),
            pltpu.VMEM(features.shape, bf16),
            pltpu.VMEM((features.shape[1], 128), f32),
            pltpu.VMEM((4 * slab, 256), bf16),
            pltpu.VMEM((40, 256), f32),
            pltpu.VMEM((40, 256), f32),
            pltpu.VMEM((rows, depth), bf16),
            pltpu.VMEM((depth, rows), bf16),
            pltpu.VMEM((4, slab, channels), f32),
            pltpu.VMEM((2, 4, slab, channels), f32),
            pltpu.VMEM((mids + 1, 2, slab, channels), f32),
            pltpu.VMEM((4, mel + 256, channels), f32),
            pltpu.VMEM((32, channels), f32),
            pltpu.VMEM((blocks, rows, width), bf16),
            pltpu.VMEM(proj_weight.shape, bf16),
            pltpu.VMEM(qkv_weight.shape, bf16),
            pltpu.VMEM(out_weight.shape, bf16),
            pltpu.VMEM((blocks, rows, width), bf16),
            pltpu.VMEM((blocks * rows, width), bf16),
            pltpu.VMEM((blocks * rows, 3 * width), bf16),
            pltpu.VMEM((rows, width), bf16),
            pltpu.VMEM((rows, 3 * width), bf16),
            pltpu.VMEM((rows, blocks * rows), f32),
            pltpu.VMEM((blocks, 2 * HEADS, rows), f32),
            pltpu.VMEM((rows, width), f32),
            pltpu.VMEM((count, half, rows, PANEL), bf16),
            pltpu.VMEM((2 * share, half * rows), bf16),
            pltpu.VMEM((count, share, PANEL), bf16),
            pltpu.VMEM((count, share, PANEL), bf16),
            dma((13,)),
            dma((2,)),
            dma((2 + 4 * PIECES,)),
            dma((2 + 4 * PIECES,)),
            dma((2 + 4 * PIECES,)),
            dma((2 + 4 * PIECES,)),
            dma((blocks,)),
            dma((blocks,)),
            dma((2, half)),
            dma((2, half)),
            dma((count, 4 * steps)),
            dma((count, 4 * steps)),
            dma((count,)),
            dma((count,)),
            dma((4,)),
        ],
        compiler_params=pltpu.CompilerParams(
            vmem_limit_bytes=58 * 1024 * 1024, collective_id=1, has_side_effects=True
        ),
        name="core",
    )(
        gain,
        bounds,
        live,
        features,
        stem_kernel,
        mid_depthwise,
        mid_pointwise,
        last_depthwise,
        last_pointwise,
        cotangent,
        proj_weight,
        qkv_weight,
        out_weight,
    )


def per_device(
    size,
    features,
    stem_kernel,
    mid_depthwise,
    mid_pointwise,
    last_depthwise,
    last_pointwise,
    proj_weight,
    norm_gain,
    qkv_weight,
    out_weight,
    cotangent,
    utt_bounds,
    live_blocks,
):
    results = core(
        size,
        features.T,
        norm_gain.reshape(1, -1),
        utt_bounds.T,
        live_blocks,
        stem_kernel,
        mid_depthwise,
        mid_pointwise,
        last_depthwise,
        last_pointwise,
        cotangent,
        proj_weight,
        qkv_weight,
        out_weight,
    )
    return finished(results)


def solution(mesh):
    split = P(("groups", "tm"), None)
    in_specs = (split,) + (P(),) * 9 + (split, P("groups", None), split)
    return jax.shard_map(
        functools.partial(per_device, mesh.shape["tm"]),
        mesh=mesh,
        in_specs=in_specs,
        out_specs=(split, split, split),
        check_vma=False,
    )
```
